256 devices in a mesh: mem: 8 (over x, core), band: 32 (over y, z).
Axes of the slice: x: 4, y: 4, z: 8, core: 2. Of those that a mesh axis runs over, the one named last changes fastest.
Arguments:
- sample_collection: float32 [48, 3, 256, 4096], P('mem', None, 'band'), may hold values from -6 to 6
- seabed_profile: float32 [256, 4096], P('band'), may hold values from 0.5 to 2
- gauge_grid_position: int32 [128, 128], P('band'), may hold values from 0 to 1048575, as said below
- observed_values: float32 [128, 128], P('band'), may hold values from -6 to 6
- error_scale: float32 [128, 128], P('band'), may hold values from 0.3 to 3
- perturbation: float32 [48, 128, 128], P('mem', 'band'), may hold values from -6 to 6
- inflation: float32 [1], replicated, may hold values from 1 to 16
Outputs:
- analysis: float32 [48, 3, 256, 4096], P('mem', None, 'band')
The draws below stay inside these ranges and needn't reach their ends.
Inputs may be any that keep to these rules, and one draw needn't show every extreme that they name: Every entry in row r of gauge_grid_position lies in grid rows b * 8 to (b + 1) * 8 - 1 with b = r // 4; cells may repeat.
All inputs are finite; a program needn't handle non-finite values.
Results may differ from the reference program's by a relative error of at most 0.000071.
Values sent between devices are 32-bit elements; how exact they have to be, the bound alone decides.
A program may use at most 128 MiB of HBM per device.

```python
import math
import jax
import jax.numpy as jnp
from jax import lax

ROWS = 8
NC = 4096
OBS_ROWS_DEV = 4
STEPS = 2
MEMBERS = 48
NY = 256
OBS_ROWS = 128


def draw_gauge_grid_position(key, part):
    band_of_row = jnp.arange(OBS_ROWS, dtype=jnp.int32) // OBS_ROWS_DEV
    offsets = jax.random.randint(key, (OBS_ROWS, 128), 0, ROWS * NC, dtype=jnp.int32)
    return band_of_row[:, None] * (ROWS * NC) + offsets


def shard_levels(key, extent, pieces, low, largest):
    loudness = 1.0
    for dim, parts in pieces:
        steps = jax.random.uniform(jax.random.fold_in(jax.random.fold_in(key, 6), dim), (parts,), jnp.float32, low / len(pieces), largest / len(pieces))
        loudness = loudness * jnp.repeat(jnp.exp(steps), extent[dim] // parts).reshape((-1,) + (1,) * (len(extent) - 1 - dim))
    return loudness


def noise(rng, shape, width, most, pieces=(), kind=jnp.bfloat16):
    entries = jax.random.normal(rng, shape, jnp.float32) * width
    if len(pieces) > 0:
        entries = shard_levels(rng, shape, pieces, -0.22, 0.18) * entries
    return jnp.clip(entries, min=-most, max=most).astype(kind)


def setup_inputs(seed: int = 0) -> dict:
    seeds = jax.random.split(jax.random.key(seed), 8)
    return {
        "sample_collection": noise(seeds[0], (MEMBERS, 3, NY, NC), 1.0, 6.0, ((0, 8), (2, 32)), jnp.float32),
        "seabed_profile": jnp.clip(jnp.exp(math.log(2.0) - 1.3862944 * jax.random.uniform(seeds[1], (NY, NC), jnp.float32) ** shard_levels(seeds[1], (NY, NC), ((0, 32),), -0.2, 0.2)), 0.5, 2.0),
        "gauge_grid_position": draw_gauge_grid_position(jax.random.fold_in(seeds[7], 71), 0),
        "observed_values": noise(seeds[3], (OBS_ROWS, 128), 1.0, 6.0, ((0, 32),), jnp.float32),
        "error_scale": jnp.clip(jnp.exp(math.log(3.0) - 2.3025851 * jax.random.uniform(seeds[4], (OBS_ROWS, 128), jnp.float32) ** shard_levels(seeds[4], (OBS_ROWS, 128), ((0, 32),), -0.2, 0.2)), 0.3, 3.0),
        "perturbation": noise(seeds[5], (MEMBERS, OBS_ROWS, 128), 1.0, 6.0, ((0, 8), (1, 32)), jnp.float32),
        "inflation": jnp.clip(jnp.exp(jax.random.uniform(seeds[6], (1,), jnp.float32, math.log(1.0), math.log(16.0))), 1.0, 16.0),
    }


courant = 0.5
coriolis_base = 0.15
coriolis_slope = 0.3

def east_diff(quantity):
    return (jnp.roll(quantity, -1, axis=-1) - jnp.roll(quantity, 1, axis=-1)) * 0.5

def north_diff(quantity):
    padded = jnp.pad(quantity, ((1, 1), (0, 0)))
    return (padded[2:] - padded[:-2]) * 0.5

def advance_one_sample(sample_trajectory, seabed_profile, earth_spin_turning):
    surface_height, eastward_velocity_field, northward_velocity_field = (sample_trajectory[0], sample_trajectory[1], sample_trajectory[2])
    for _ in range(STEPS):
        surface_height = surface_height - courant * (east_diff(seabed_profile * eastward_velocity_field) + north_diff(seabed_profile * northward_velocity_field))
        eastward_velocity_field = eastward_velocity_field - courant * east_diff(surface_height) + earth_spin_turning * northward_velocity_field
        northward_velocity_field = northward_velocity_field - courant * north_diff(surface_height) - earth_spin_turning * eastward_velocity_field
    return jnp.stack([surface_height, eastward_velocity_field, northward_velocity_field])

def reference(sample_collection, seabed_profile, gauge_grid_position, observed_values, error_scale, perturbation, inflation):
    sample_trajectories = sample_collection.shape[0]
    rows_index = jnp.arange(NY).astype(jnp.float32)
    earth_spin_turning = (coriolis_base + coriolis_slope * (rows_index + 0.5) / NY)[:, None]
    prior_model_outputs = lax.map(lambda sample_trajectory: advance_one_sample(sample_trajectory, seabed_profile, earth_spin_turning), sample_collection)
    modelled_water_levels = jnp.take(prior_model_outputs[:, 0].reshape(sample_trajectories, -1), gauge_grid_position.reshape(-1), axis=1)
    obs_scale = error_scale.reshape(-1)
    factor = inflation[0]
    innovation = (observed_values.reshape(-1) + jnp.sqrt(factor) * obs_scale * perturbation.reshape(sample_trajectories, -1) - modelled_water_levels) / obs_scale
    centre = lax.optimization_barrier(jnp.sum(modelled_water_levels, axis=0)) / sample_trajectories
    spread = (modelled_water_levels - centre) / (obs_scale * math.sqrt(sample_trajectories - 1))
    gram_matrix = jnp.dot(spread.astype(jnp.float32), spread.T.astype(jnp.float32), precision=lax.Precision.HIGHEST, preferred_element_type=jnp.float32)
    cross_term = jnp.dot(spread.astype(jnp.float32), innovation.T.astype(jnp.float32), precision=lax.Precision.HIGHEST, preferred_element_type=jnp.float32)
    system = gram_matrix + factor * jnp.eye(sample_trajectories, dtype=jnp.float32)
    cholesky_lower = jnp.linalg.cholesky(system)
    middle = lax.linalg.triangular_solve(cholesky_lower, cross_term, left_side=True, lower=True)
    weights = lax.linalg.triangular_solve(cholesky_lower, middle, left_side=True, lower=True, transpose_a=True)
    assimilate_update_step = jnp.eye(sample_trajectories, dtype=jnp.float32) + (weights - lax.optimization_barrier(jnp.mean(weights, axis=0, keepdims=True))) / math.sqrt(sample_trajectories - 1)
    return jnp.tensordot(assimilate_update_step, prior_model_outputs, axes=([0], [0]), precision=lax.Precision.HIGHEST)
```

```python
import functools
import math

import jax
import jax.numpy as jnp
from jax import lax
from jax.experimental import pallas as pl
from jax.experimental.pallas import tpu as pltpu
from jax.sharding import PartitionSpec as P

MESH = pl.DeviceIdType.MESH
HIGHEST = lax.Precision.HIGHEST

coriolis_base = 0.15
coriolis_slope = 0.3
PAD = 8


def rows_of(shape):
    return lax.broadcasted_iota(jnp.int32, shape, 0)


def lanes_of(shape):
    return lax.broadcasted_iota(jnp.int32, shape, 1)


def east(q):
    n = q.shape[1]
    return pltpu.roll(q, n - 1, 1) - pltpu.roll(q, 1, 1)


def north(q, above, below):
    n = q.shape[0]
    row = rows_of(q.shape)
    after = jnp.where(row == n - 1, below, pltpu.roll(q, n - 1, 0))
    before = jnp.where(row == 0, above, pltpu.roll(q, 1, 0))
    return after - before


def nt(a, b, precision=None):
    return lax.dot_general(
        a, b, (((1,), (1,)), ((), ())), precision=precision, preferred_element_type=jnp.float32
    )


def kernel(
    nm, nb, gz,
    ens, depth, pos, obs, scale, pert, infl,
    out,
    st, dv, hs, hr, onehot, hb, pi, zb, yb, xb, mb, spread_rows,
    load_sem, hs_sem, hr_sem, as_sem, ar_sem, zs_sem, zr_sem, ys_sem, yr_sem,
    fs_sem, fr_sem, bs_sem, br_sem,
):
    _, members, rows, cols = st.shape
    n_obs = onehot.shape[1]
    width = cols // nm
    np_ = nm * PAD
    total = nm * members
    cells = total * rows
    gy = nb // gz
    norm = math.sqrt(total - 1)
    me, b = lax.axis_index("mem"), lax.axis_index("band")
    z, y = lax.rem(b, gz), lax.div(b, gz)

    @pl.loop(0, members)
    def _(m):
        pltpu.make_async_copy(ens.at[m], st.at[:, m], load_sem.at[m]).start()

    barrier = pltpu.get_barrier_semaphore()
    for s in range(1, nm):
        pl.semaphore_signal(barrier, 1, device_id={"mem": lax.rem(me + s, nm)}, device_id_type=MESH)
    for s in range(1, gz):
        peer = y * gz + lax.rem(z + s, gz)
        pl.semaphore_signal(barrier, 1, device_id={"band": peer}, device_id_type=MESH)
    for s in range(1, gy):
        peer = lax.rem(y + s, gy) * gz + z
        pl.semaphore_signal(barrier, 1, device_id={"band": peer}, device_id_type=MESH)
    far_above = jnp.logical_and(z == 0, y > 0)
    far_below = jnp.logical_and(z == gz - 1, y < gy - 1)

    @pl.when(far_above)
    def _():
        pl.semaphore_signal(barrier, 1, device_id={"band": b - 1}, device_id_type=MESH)

    @pl.when(far_below)
    def _():
        pl.semaphore_signal(barrier, 1, device_id={"band": b + 1}, device_id_type=MESH)

    @pl.when(b == 0)
    def _():
        hr[:, 0] = jnp.zeros_like(hr[:, 0])

    @pl.when(b == nb - 1)
    def _():
        hr[:, 1] = jnp.zeros_like(hr[:, 1])

    def flat(x):
        return jnp.concatenate([x[q : q + 1, :] for q in range(x.shape[0])], axis=1)

    local = flat(pos[...]) - b * (rows * cols)
    obs_row = lax.shift_right_logical(local, int(math.log2(cols)))
    obs_col = jnp.bitwise_and(local, cols - 1)
    step = 256

    @pl.loop(0, cols // step)
    def _(k):
        col = rows_of((step, n_obs)) + k * step
        onehot[pl.ds(pl.multiple_of(k * step, step), step), :] = jnp.where(
            col == obs_col, 1.0, 0.0
        ).astype(jnp.bfloat16)

    j = lax.shift_right_logical(rows_of((cells, np_)), int(math.log2(rows)))
    padded = j
    for k in range(1, nm):
        padded = padded + jnp.where(j >= k * members, PAD - members, 0)
    spread_rows[...] = jnp.where(lanes_of((cells, np_)) == padded, 1.0, 0.0).astype(jnp.bfloat16)

    turn = coriolis_base + coriolis_slope * (
        (rows_of((rows, cols)) + b * rows).astype(jnp.float32) + 0.5
    ) / (nb * rows)
    inner_above = jnp.where(b > 0, 0.25, 0.0)
    inner_below = jnp.where(b < nb - 1, 0.25, 0.0)

    pl.semaphore_wait(
        barrier,
        nm - 1 + gz - 1 + gy - 1 + jnp.where(far_above, 1, 0) + jnp.where(far_below, 1, 0),
    )

    def halo(t, side, m):
        return pltpu.make_async_remote_copy(
            src_ref=hs.at[t, side, m],
            dst_ref=hr.at[t, 1 - side, m],
            send_sem=hs_sem.at[t, side, m],
            recv_sem=hr_sem.at[t, 1 - side, m],
            device_id={"band": jnp.where(b > 0, b - 1, 0) if side == 0 else jnp.where(b < nb - 1, b + 1, b)},
            device_id_type=MESH,
        )

    def begin(t, m, h, u, v):
        d = depth[...]
        flux = d * v
        part = h - 0.25 * east(d * u)
        dv[m] = flux
        st[0, m] = part
        hs[t, 0, m, 0:1, :] = flux[0:1]
        hs[t, 0, m, 1:2, :] = part[0:1] - 0.25 * flux[1:2]
        hs[t, 1, m, 0:1, :] = flux[rows - 1 : rows]
        hs[t, 1, m, 1:2, :] = part[rows - 1 : rows] + 0.25 * flux[rows - 2 : rows - 1]

        @pl.when(b > 0)
        def _():
            halo(t, 0, m).start()

        @pl.when(b < nb - 1)
        def _():
            halo(t, 1, m).start()

    def arrive(t, m):
        @pl.when(b > 0)
        def _():
            halo(t, 1, m).wait_recv()

        @pl.when(b < nb - 1)
        def _():
            halo(t, 0, m).wait_recv()

    def new_height(t, m):
        return st[0, m] - 0.25 * north(dv[m], hr[t, 0, m, 0:1, :], hr[t, 1, m, 0:1, :])

    def new_flow(t, m, h):
        flux = dv[m]
        above = hr[t, 0, m, 1:2, :] - inner_above * flux[0:1]
        below = hr[t, 1, m, 1:2, :] + inner_below * flux[rows - 1 : rows]
        v = st[2, m]
        u = st[1, m] - 0.25 * east(h) + turn * v
        v = v - 0.25 * north(h, above, below) - turn * u
        return u, v

    @pl.loop(0, members)
    def _(m):
        pltpu.make_async_copy(ens.at[m], st.at[:, m], load_sem.at[m]).wait()
        begin(0, m, st[0, m], st[1, m], st[2, m])

    @pl.loop(0, members)
    def _(m):
        arrive(0, m)
        h = new_height(0, m)
        u, v = new_flow(0, m, h)
        st[1, m] = u
        st[2, m] = v
        begin(1, m, h, u, v)

    @pl.loop(0, members)
    def _(m):
        arrive(1, m)
        st[0, m] = new_height(1, m)

    tall = members * rows
    kstep = 512

    def pick(k, acc):
        at = pl.ds(pl.multiple_of(k * kstep, kstep), kstep)
        h = st[0, :, :, at].reshape(tall, kstep)
        hi = h.astype(jnp.bfloat16)
        rest = h - hi.astype(jnp.float32)
        mid = rest.astype(jnp.bfloat16)
        low = (rest - mid.astype(jnp.float32)).astype(jnp.bfloat16)
        hb[0:tall] = hi
        hb[tall : 2 * tall] = mid
        hb[2 * tall : 3 * tall] = low
        return acc + jnp.dot(hb[...], onehot[at, :], preferred_element_type=jnp.float32)

    picked = lax.fori_loop(0, cols // kstep, pick, jnp.zeros((3 * tall, n_obs), jnp.float32))
    picked = picked[0:tall] + (picked[tall : 2 * tall] + picked[2 * tall : 3 * tall])
    here = rows_of((rows, n_obs)) == obs_row
    slot = rows_of((PAD, n_obs))
    predicted = jnp.zeros((PAD, n_obs), jnp.float32)
    noise = jnp.zeros((PAD, n_obs), jnp.float32)
    for m in range(members):
        mine = jnp.where(here, picked[m * rows : (m + 1) * rows], 0.0)
        predicted = jnp.where(slot == m, jnp.sum(mine, axis=0, keepdims=True), predicted)
        noise = jnp.where(slot == m, flat(pert[m]), noise)
    err = flat(scale[...])
    factor = jnp.full((1, n_obs), infl[0], jnp.float32)
    innovation = (flat(obs[...]) + jnp.sqrt(factor) * err * noise - predicted) / err
    pi[me, 0] = predicted
    pi[me, 1] = jnp.where(slot < members, innovation, 0.0)

    def gather(peer, src):
        return pltpu.make_async_remote_copy(
            src_ref=pi.at[src], dst_ref=pi.at[src], send_sem=as_sem.at[peer],
            recv_sem=ar_sem.at[src], device_id={"mem": peer}, device_id_type=MESH,
        )

    for s in range(1, nm):
        gather(lax.rem(me + s, nm), me).start()

    @pl.loop(0, members)
    def _(m):
        u, v = new_flow(1, m, st[0, m])
        st[1, m] = u
        st[2, m] = v

    own = pl.ds(pl.multiple_of(me * width, width), width)

    def forth(f, peer, src):
        at = pl.ds(pl.multiple_of(peer * width, width), width)
        return pltpu.make_async_remote_copy(
            src_ref=st.at[f, :, :, at], dst_ref=xb.at[f, src], send_sem=fs_sem.at[f, peer],
            recv_sem=fr_sem.at[f, src], device_id={"mem": peer}, device_id_type=MESH,
        )

    for f in range(3):
        for s in range(1, nm):
            forth(f, lax.rem(me + s, nm), me).start()
    for f in range(3):
        xb[f, me] = st[f, :, :, own]

    for s in range(1, nm):
        src = lax.rem(me + s, nm)
        gather(src, src).wait_recv()
    predicted = pi[:, 0].reshape(np_, n_obs)
    centre = jnp.sum(predicted, axis=0, keepdims=True) * (1.0 / total)
    inside = jnp.bitwise_and(rows_of((np_, n_obs)), PAD - 1) < members
    spread = jnp.where(inside, (predicted - centre) / (err * norm), 0.0)
    both = jnp.concatenate([spread, pi[:, 1].reshape(np_, n_obs)], axis=0)
    zb[z] = nt(spread, both, HIGHEST)

    def share(buf, send, recv, slot_, peer_slot, peer):
        return pltpu.make_async_remote_copy(
            src_ref=buf.at[slot_], dst_ref=buf.at[slot_], send_sem=send.at[peer_slot],
            recv_sem=recv.at[slot_], device_id={"band": peer}, device_id_type=MESH,
        )

    for s in range(1, gz):
        other = lax.rem(z + s, gz)
        share(zb, zs_sem, zr_sem, z, other, y * gz + other).start()
    for s in range(1, gz):
        other = lax.rem(z + s, gz)
        share(zb, zs_sem, zr_sem, other, other, y * gz + other).wait_recv()
    yb[y] = jnp.sum(zb[...], axis=0)
    for s in range(1, gy):
        other = lax.rem(y + s, gy)
        share(yb, ys_sem, yr_sem, y, other, other * gz + z).start()
    for s in range(1, gy):
        other = lax.rem(y + s, gy)
        share(yb, ys_sem, yr_sem, other, other, other * gz + z).wait_recv()
    system = jnp.sum(yb[...], axis=0)
    shape = (np_, 2 * np_)
    system = system + jnp.where(rows_of(shape) == lanes_of(shape), infl[0], 0.0)

    blocks = [system[k * PAD : (k + 1) * PAD] for k in range(nm)]
    sub = rows_of((PAD, 2 * np_))
    for k in range(total):
        home, r = divmod(k, members)
        p = home * PAD + r
        line = blocks[home][r : r + 1]
        line = line / line[:, p : p + 1]
        new = [x - x[:, p : p + 1] * line for x in blocks]
        new[home] = jnp.where(sub == r, line, new[home])
        blocks = new
    weights = jnp.concatenate([x[:, np_:] for x in blocks], axis=0)
    square = (np_, np_)
    mean = jnp.sum(weights, axis=0, keepdims=True) * (1.0 / total)
    transform = jnp.where(rows_of(square) == lanes_of(square), 1.0, 0.0) + (weights - mean) * (1.0 / norm)

    alike = jnp.bitwise_and(rows_of((cells, cells)), rows - 1) == jnp.bitwise_and(
        lanes_of((cells, cells)), rows - 1
    )

    def widen(t):
        grown = nt(spread_rows[...], t).astype(jnp.bfloat16)
        return jnp.where(alike, nt(grown, spread_rows[...]), 0.0).astype(jnp.bfloat16)

    hi = transform.astype(jnp.bfloat16)
    mix_hi = widen(hi)
    mix_lo = widen((transform - hi.astype(jnp.float32)).astype(jnp.bfloat16))

    def back(f, peer, src):
        at = pl.ds(pl.multiple_of(src * width, width), width)
        return pltpu.make_async_remote_copy(
            src_ref=mb.at[f, peer], dst_ref=out.at[:, f, :, at], send_sem=bs_sem.at[f, peer],
            recv_sem=br_sem.at[f, src], device_id={"mem": peer}, device_id_type=MESH,
        )

    for f in range(3):
        for s in range(1, nm):
            src = lax.rem(me + s, nm)
            forth(f, src, src).wait_recv()
        x = xb[f].reshape(cells, width)
        x_hi = x.astype(jnp.bfloat16)
        x_lo = (x - x_hi.astype(jnp.float32)).astype(jnp.bfloat16)
        mixed = jnp.dot(mix_hi, x_hi, preferred_element_type=jnp.float32) + (
            jnp.dot(mix_hi, x_lo, preferred_element_type=jnp.float32)
            + jnp.dot(mix_lo, x_hi, preferred_element_type=jnp.float32)
        )
        mb[f] = mixed.reshape(nm, members, rows, width)
        for s in range(1, nm):
            back(f, lax.rem(me + s, nm), me).start()
        out[:, f, :, own] = mb[f, me]

    @pl.loop(0, members)
    def _(m):
        for t in range(2):

            @pl.when(b > 0)
            def _():
                halo(t, 0, m).wait_send()

            @pl.when(b < nb - 1)
            def _():
                halo(t, 1, m).wait_send()

    for s in range(1, nm):
        gather(lax.rem(me + s, nm), me).wait_send()
    for s in range(1, gz):
        other = lax.rem(z + s, gz)
        share(zb, zs_sem, zr_sem, z, other, y * gz + other).wait_send()
    for s in range(1, gy):
        other = lax.rem(y + s, gy)
        share(yb, ys_sem, yr_sem, y, other, other * gz + z).wait_send()
    for f in range(3):
        for s in range(1, nm):
            peer = lax.rem(me + s, nm)
            forth(f, peer, me).wait_send()
    for f in range(3):
        for s in range(1, nm):
            peer = lax.rem(me + s, nm)
            back(f, peer, me).wait_send()
            back(f, peer, peer).wait_recv()


def body(ens, depth, pos, obs, scale, pert, infl):
    nm, nb = lax.axis_size("mem"), lax.axis_size("band")
    gz = 8 if nb >= 16 else 2
    gy = nb // gz
    members, fields, rows, cols = ens.shape
    n_obs = pos.size
    np_ = nm * PAD
    cells = nm * members * rows
    f32, bf16 = jnp.float32, jnp.bfloat16
    dma = pltpu.SemaphoreType.DMA
    vmem = pl.BlockSpec(memory_space=pltpu.VMEM)
    return pl.pallas_call(
        functools.partial(kernel, nm, nb, gz),
        out_shape=jax.ShapeDtypeStruct(ens.shape, f32),
        in_specs=[pl.BlockSpec(memory_space=pl.ANY)] + [vmem] * 5 + [pl.BlockSpec(memory_space=pltpu.SMEM)],
        out_specs=vmem,
        scratch_shapes=[
            pltpu.VMEM((fields, members, rows, cols), f32),
            pltpu.VMEM((members, rows, cols), f32),
            pltpu.VMEM((2, 2, members, 2, cols), f32),
            pltpu.VMEM((2, 2, members, 2, cols), f32),
            pltpu.VMEM((cols, n_obs), bf16),
            pltpu.VMEM((3 * members * rows, 512), bf16),
            pltpu.VMEM((nm, 2, PAD, n_obs), f32),
            pltpu.VMEM((gz, np_, 2 * np_), f32),
            pltpu.VMEM((gy, np_, 2 * np_), f32),
            pltpu.VMEM((fields, nm, members, rows, cols // nm), f32),
            pltpu.VMEM((fields, nm, members, rows, cols // nm), f32),
            pltpu.VMEM((cells, np_), bf16),
            dma((members,)),
            dma((2, 2, members)),
            dma((2, 2, members)),
            dma((nm,)),
            dma((nm,)),
            dma((gz,)),
            dma((gz,)),
            dma((gy,)),
            dma((gy,)),
            dma((fields, nm)),
            dma((fields, nm)),
            dma((fields, nm)),
            dma((fields, nm)),
        ],
        compiler_params=pltpu.CompilerParams(
            collective_id=0, has_side_effects=True, vmem_limit_bytes=48 * 1024 * 1024
        ),
        name="smoother",
    )(ens, depth, pos, obs, scale, pert, infl)


def solution(mesh):
    in_specs = (
        P("mem", None, "band", None),
        P("band", None),
        P("band", None),
        P("band", None),
        P("band", None),
        P("mem", "band", None),
        P(),
    )
    out_specs = P("mem", None, "band", None)
    return jax.shard_map(body, mesh=mesh, in_specs=in_specs, out_specs=out_specs, check_vma=False)
```

```python
import functools
import math

import jax
import jax.numpy as jnp
from jax import lax
from jax.experimental import pallas as pl
from jax.experimental.pallas import tpu as pltpu
from jax.sharding import PartitionSpec as P

MESH = pl.DeviceIdType.MESH
HIGHEST = lax.Precision.HIGHEST

coriolis_base = 0.15
coriolis_slope = 0.3
PAD = 8


def rows_of(shape):
    return lax.broadcasted_iota(jnp.int32, shape, 0)


def lanes_of(shape):
    return lax.broadcasted_iota(jnp.int32, shape, 1)


def east(q):
    n = q.shape[1]
    return pltpu.roll(q, n - 1, 1) - pltpu.roll(q, 1, 1)


def north(q, above, below):
    n = q.shape[0]
    row = rows_of(q.shape)
    after = jnp.where(row == n - 1, below, pltpu.roll(q, n - 1, 0))
    before = jnp.where(row == 0, above, pltpu.roll(q, 1, 0))
    return after - before


def nt(a, b, precision=None):
    return lax.dot_general(
        a, b, (((1,), (1,)), ((), ())), precision=precision, preferred_element_type=jnp.float32
    )


def kernel(
    nm, nb, gz,
    ens, depth_in, pos_in, obs_in, scale_in, pert_in, infl,
    out,
    depth, pos, obs, scale, pert,
    st, dv, hs, hr, onehot, hb, noise, pi, zb, yb, sb, xb, mb, spread_rows,
    load_sem, small_sem, hs_sem, hr_sem, ns_sem, nr_sem, as_sem, ar_sem, zs_sem, zr_sem, ys_sem, yr_sem,
    ss_sem, sr_sem, fs_sem, fr_sem, bs_sem, br_sem,
):
    _, members, rows, cols = st.shape
    n_obs = onehot.shape[1]
    width = cols // nm
    np_ = nm * PAD
    total = nm * members
    cells = total * rows
    gy = nb // gz
    norm = math.sqrt(total - 1)
    H, U, V = 0, 1, 2
    me, b = lax.axis_index("mem"), lax.axis_index("band")
    z, y = lax.rem(b, gz), lax.div(b, gz)
    mates = [lax.rem(me + s, nm) for s in range(1, nm)]

    small = [
        pltpu.make_async_copy(source, target, small_sem.at[k])
        for k, (source, target) in enumerate(
            [(depth_in, depth), (pos_in, pos), (obs_in, obs), (scale_in, scale), (pert_in, pert)]
        )
    ]
    load = [pltpu.make_async_copy(ens.at[:, f], st.at[f], load_sem.at[f]) for f in range(3)]
    small[0].start()
    load[V].start()
    small[4].start()
    load[U].start()
    load[H].start()
    for copy in small[1:4]:
        copy.start()

    barrier = pltpu.get_barrier_semaphore()

    def greet(where):
        pl.semaphore_signal(barrier, 1, device_id=where, device_id_type=MESH)

    for peer in mates:
        greet({"mem": peer})
    for s in range(1, gz):
        greet({"band": y * gz + lax.rem(z + s, gz)})
    for s in range(1, gy):
        greet({"band": lax.rem(y + s, gy) * gz + z})
    far_above = jnp.logical_and(z == 0, y > 0)
    far_below = jnp.logical_and(z == gz - 1, y < gy - 1)

    @pl.when(far_above)
    def _():
        greet({"band": b - 1})

    @pl.when(far_below)
    def _():
        greet({"band": b + 1})

    @pl.when(b == 0)
    def _():
        hr[:, 0] = jnp.zeros_like(hr[:, 0])

    @pl.when(b == nb - 1)
    def _():
        hr[:, 1] = jnp.zeros_like(hr[:, 1])

    def turn(lanes):
        row = (rows_of((rows, lanes)) + b * rows).astype(jnp.float32)
        return coriolis_base + coriolis_slope * (row + 0.5) / (nb * rows)

    def halo(t, side, m):
        return pltpu.make_async_remote_copy(
            src_ref=hs.at[t, side, m],
            dst_ref=hr.at[t, 1 - side, m],
            send_sem=hs_sem.at[t, side, m],
            recv_sem=hr_sem.at[t, 1 - side, m],
            device_id={"band": jnp.where(b > 0, b - 1, 0) if side == 0 else jnp.where(b < nb - 1, b + 1, b)},
            device_id_type=MESH,
        )

    def edges(t, m, q):
        hs[t, 0, m] = q[0:1]
        hs[t, 1, m] = q[rows - 1 : rows]

        @pl.when(b > 0)
        def _():
            halo(t, 0, m).start()

        @pl.when(b < nb - 1)
        def _():
            halo(t, 1, m).start()

    def arrive(t, m):
        @pl.when(b > 0)
        def _():
            halo(t, 1, m).wait_recv()

        @pl.when(b < nb - 1)
        def _():
            halo(t, 0, m).wait_recv()

    def tell(buf, send, recv, peer, src):
        return pltpu.make_async_remote_copy(
            src_ref=buf.at[src], dst_ref=buf.at[src], send_sem=send.at[peer],
            recv_sem=recv.at[src], device_id={"mem": peer}, device_id_type=MESH,
        )

    def share(buf, send, recv, slot, other, peer):
        return pltpu.make_async_remote_copy(
            src_ref=buf.at[slot], dst_ref=buf.at[slot], send_sem=send.at[other],
            recv_sem=recv.at[slot], device_id={"band": peer}, device_id_type=MESH,
        )

    def columns(peer):
        return pl.ds(pl.multiple_of(peer * width, width), width)

    def forth(f, peer, src):
        return pltpu.make_async_remote_copy(
            src_ref=st.at[f, :, :, columns(peer)], dst_ref=xb.at[f, src], send_sem=fs_sem.at[f, peer],
            recv_sem=fr_sem.at[f, src], device_id={"mem": peer}, device_id_type=MESH,
        )

    def forth_one(f, m, peer):
        return pltpu.make_async_remote_copy(
            src_ref=st.at[f, m, :, columns(peer)], dst_ref=xb.at[f, me, m], send_sem=fs_sem.at[f, peer],
            recv_sem=fr_sem.at[f, me], device_id={"mem": peer}, device_id_type=MESH,
        )

    def back(f, peer, src):
        return pltpu.make_async_remote_copy(
            src_ref=mb.at[f, peer], dst_ref=out.at[:, f, :, columns(src)], send_sem=bs_sem.at[f, peer],
            recv_sem=br_sem.at[f, src], device_id={"mem": peer}, device_id_type=MESH,
        )

    pl.semaphore_wait(
        barrier,
        nm - 1 + gz - 1 + gy - 1 + jnp.where(far_above, 1, 0) + jnp.where(far_below, 1, 0),
    )

    small[0].wait()
    load[V].wait()

    @pl.loop(0, members)
    def _(m):
        flux = depth[...] * st[V, m]
        dv[m] = flux
        edges(0, m, flux)

    def flat(x):
        return jnp.concatenate([x[q : q + 1, :] for q in range(x.shape[0])], axis=1)

    small[4].wait()
    slot = rows_of((PAD, n_obs))
    own_noise = jnp.zeros((PAD, n_obs), jnp.float32)
    for m in range(members):
        own_noise = jnp.where(slot == m, flat(pert[m]), own_noise)
    noise[me] = own_noise
    for peer in mates:
        tell(noise, ns_sem, nr_sem, peer, me).start()

    load[U].wait()
    load[H].wait()

    @pl.loop(0, members)
    def _(m):
        st[H, m] = st[H, m] - 0.25 * east(depth[...] * st[U, m])

    @pl.loop(0, members)
    def _(m):
        arrive(0, m)
        h = st[H, m] - 0.25 * north(dv[m], hr[0, 0, m], hr[0, 1, m])
        st[H, m] = h
        edges(1, m, h)
        st[U, m] = st[U, m] - 0.25 * east(h) + turn(cols) * st[V, m]
        for peer in mates:
            forth_one(U, m, peer).start()

    for copy in small[1:4]:
        copy.wait()

    local = flat(pos[...]) - b * (rows * cols)
    obs_row = lax.shift_right_logical(local, int(math.log2(cols)))
    obs_col = jnp.bitwise_and(local, cols - 1)
    step = 256

    @pl.loop(0, cols // step)
    def _(k):
        col = rows_of((step, n_obs)) + k * step
        onehot[pl.ds(pl.multiple_of(k * step, step), step), :] = jnp.where(
            col == obs_col, 1.0, 0.0
        ).astype(jnp.bfloat16)

    @pl.loop(0, members)
    def _(m):
        arrive(1, m)
        v = st[V, m] - 0.25 * north(st[H, m], hr[1, 0, m], hr[1, 1, m]) - turn(cols) * st[U, m]
        st[V, m] = v
        flux = depth[...] * v
        dv[m] = flux
        edges(2, m, flux)

    @pl.loop(0, members)
    def _(m):
        h = st[H, m] - 0.25 * east(depth[...] * st[U, m])
        arrive(2, m)
        st[H, m] = h - 0.25 * north(dv[m], hr[2, 0, m], hr[2, 1, m])

    tall = members * rows
    kstep = 512

    def pick(k, acc):
        at = pl.ds(pl.multiple_of(k * kstep, kstep), kstep)
        h = st[H, :, :, at].reshape(tall, kstep)
        hi = h.astype(jnp.bfloat16)
        rest = h - hi.astype(jnp.float32)
        mid = rest.astype(jnp.bfloat16)
        low = (rest - mid.astype(jnp.float32)).astype(jnp.bfloat16)
        hb[0:tall] = hi
        hb[tall : 2 * tall] = mid
        hb[2 * tall : 3 * tall] = low
        return acc + jnp.dot(hb[...], onehot[at, :], preferred_element_type=jnp.float32)

    picked = lax.fori_loop(0, cols // kstep, pick, jnp.zeros((3 * tall, n_obs), jnp.float32))
    picked = picked[0:tall] + (picked[tall : 2 * tall] + picked[2 * tall : 3 * tall])
    here = rows_of((rows, n_obs)) == obs_row
    own = jnp.zeros((PAD, n_obs), jnp.float32)
    for m in range(members):
        mine = jnp.where(here, picked[m * rows : (m + 1) * rows], 0.0)
        own = jnp.where(slot == m, jnp.sum(mine, axis=0, keepdims=True), own)
    pi[me] = own
    for peer in mates:
        tell(pi, as_sem, ar_sem, peer, me).start()
    for f in range(3):
        xb[f, me] = st[f, :, :, columns(me)]

    j = lax.shift_right_logical(rows_of((cells, np_)), int(math.log2(rows)))
    padded = j
    for k in range(1, nm):
        padded = padded + jnp.where(j >= k * members, PAD - members, 0)
    spread_rows[...] = jnp.where(lanes_of((cells, np_)) == padded, 1.0, 0.0).astype(jnp.bfloat16)

    err = flat(scale[...])
    factor = jnp.full((1, n_obs), infl[0], jnp.float32)
    known = flat(obs[...])
    weight = jnp.sqrt(factor) * err
    for peer in mates:
        tell(noise, ns_sem, nr_sem, peer, peer).wait_recv()
    aimed = known + weight * noise[...].reshape(np_, n_obs)
    for peer in mates:
        tell(pi, as_sem, ar_sem, peer, peer).wait_recv()
    predicted = pi[...].reshape(np_, n_obs)
    centre = jnp.sum(predicted, axis=0, keepdims=True) * (1.0 / total)
    inside = jnp.bitwise_and(rows_of((np_, n_obs)), PAD - 1) < members
    unit = err * norm
    spread = jnp.where(inside, (predicted - centre) / unit, 0.0)
    innovation = jnp.where(inside, (aimed - predicted) / err, 0.0)
    half = nm // 2
    core = lax.rem(me, 2)
    mine = pi[pl.ds(core * half, half)].reshape(half * PAD, n_obs)
    own_spread = jnp.where(inside[0 : half * PAD], (mine - centre) / unit, 0.0)
    zb[z] = nt(own_spread, jnp.concatenate([spread, innovation], axis=0), HIGHEST)
    others = [lax.rem(z + s, gz) for s in range(1, gz)]
    for other in others:
        share(zb, zs_sem, zr_sem, z, other, y * gz + other).start()
    for peer in mates:
        forth(V, peer, me).start()
    for peer in mates:
        forth(H, peer, me).start()
    for other in others:
        share(zb, zs_sem, zr_sem, other, other, y * gz + other).wait_recv()
    yb[y] = jnp.sum(zb[...], axis=0)
    layers = [lax.rem(y + s, gy) for s in range(1, gy)]
    for other in layers:
        share(yb, ys_sem, yr_sem, y, other, other * gz + z).start()
    for other in layers:
        share(yb, ys_sem, yr_sem, other, other, other * gz + z).wait_recv()
    sb[core] = jnp.sum(yb[...], axis=0)
    swap = pltpu.make_async_remote_copy(
        src_ref=sb.at[core], dst_ref=sb.at[core], send_sem=ss_sem, recv_sem=sr_sem,
        device_id={"mem": me + 1 - 2 * core}, device_id_type=MESH,
    )
    swap.start()
    swap.wait()

    shape = (PAD, 2 * np_)
    sub, lane = rows_of(shape), lanes_of(shape)
    blocks = [
        sb[k // half, (k % half) * PAD : (k % half + 1) * PAD]
        + jnp.where(sub + k * PAD == lane, infl[0], 0.0)
        for k in range(nm)
    ]
    for k in range(total):
        home, r = divmod(k, members)
        p = home * PAD + r
        line = blocks[home][r : r + 1]
        line = line / line[:, p : p + 1]
        new = [x - x[:, p : p + 1] * line for x in blocks]
        new[home] = jnp.where(sub == r, line, new[home])
        blocks = new
    weights = jnp.concatenate([x[:, np_:] for x in blocks], axis=0)
    square = (np_, np_)
    mean = jnp.sum(weights, axis=0, keepdims=True) * (1.0 / total)
    transform = jnp.where(rows_of(square) == lanes_of(square), 1.0, 0.0) + (weights - mean) * (1.0 / norm)

    alike = jnp.bitwise_and(rows_of((cells, cells)), rows - 1) == jnp.bitwise_and(
        lanes_of((cells, cells)), rows - 1
    )

    def widen(t):
        grown = nt(spread_rows[...], t).astype(jnp.bfloat16)
        return jnp.where(alike, nt(grown, spread_rows[...]), 0.0).astype(jnp.bfloat16)

    hi = transform.astype(jnp.bfloat16)
    mix_hi = widen(hi)
    mix_lo = widen((transform - hi.astype(jnp.float32)).astype(jnp.bfloat16))

    for f in (U, H, V):
        for peer in mates:
            forth(f, peer, peer).wait_recv()
        x = xb[f].reshape(cells, width)
        x_hi = x.astype(jnp.bfloat16)
        x_lo = (x - x_hi.astype(jnp.float32)).astype(jnp.bfloat16)
        mixed = jnp.dot(mix_hi, x_hi, preferred_element_type=jnp.float32) + (
            jnp.dot(mix_hi, x_lo, preferred_element_type=jnp.float32)
            + jnp.dot(mix_lo, x_hi, preferred_element_type=jnp.float32)
        )
        mb[f] = mixed.reshape(nm, members, rows, width)
        if f == V:
            for peer in mates:
                back(H, peer, me).wait_send()
        for peer in mates:
            back(f, peer, me).start()
        out[:, f, :, columns(me)] = mb[f, me]

    for peer in mates:
        back(H, peer, peer).wait_recv()

    @pl.loop(0, members)
    def _(m):
        edges(3, m, out[m, H])

    for peer in mates:
        back(U, peer, peer).wait_recv()

    @pl.loop(0, members)
    def _(m):
        out[m, U] = out[m, U] - 0.25 * east(out[m, H])

    @pl.loop(0, members)
    def _(m):
        arrive(3, m)
        dv[m] = 0.25 * north(out[m, H], hr[3, 0, m], hr[3, 1, m])

    def finish(src):
        at = columns(src)
        f = turn(width)
        for m in range(members):
            v = out[m, V, :, at]
            u = out[m, U, :, at] + f * v
            out[m, U, :, at] = u
            out[m, V, :, at] = v - dv[m, :, at] - f * u

    finish(me)

    @pl.loop(1, nm)
    def _(s):
        peer = lax.rem(me + s, nm)
        back(V, peer, peer).wait_recv()
        finish(peer)

    @pl.loop(0, members)
    def _(m):
        for t in range(4):

            @pl.when(b > 0)
            def _():
                halo(t, 0, m).wait_send()

            @pl.when(b < nb - 1)
            def _():
                halo(t, 1, m).wait_send()

    for peer in mates:
        tell(noise, ns_sem, nr_sem, peer, me).wait_send()
        tell(pi, as_sem, ar_sem, peer, me).wait_send()
    for other in others:
        share(zb, zs_sem, zr_sem, z, other, y * gz + other).wait_send()
    for other in layers:
        share(yb, ys_sem, yr_sem, y, other, other * gz + z).wait_send()
    for peer in mates:
        for f in range(3):
            forth(f, peer, me).wait_send()
        back(U, peer, me).wait_send()
        back(V, peer, me).wait_send()


def body(ens, depth, pos, obs, scale, pert, infl):
    nm, nb = lax.axis_size("mem"), lax.axis_size("band")
    gz = 8 if nb >= 16 else 2
    gy = nb // gz
    members, fields, rows, cols = ens.shape
    n_obs = pos.size
    np_ = nm * PAD
    cells = nm * members * rows
    f32, bf16 = jnp.float32, jnp.bfloat16
    dma = pltpu.SemaphoreType.DMA
    vmem = pl.BlockSpec(memory_space=pltpu.VMEM)
    return pl.pallas_call(
        functools.partial(kernel, nm, nb, gz),
        out_shape=jax.ShapeDtypeStruct(ens.shape, f32),
        in_specs=[pl.BlockSpec(memory_space=pltpu.HBM)] * 6 + [pl.BlockSpec(memory_space=pltpu.SMEM)],
        out_specs=vmem,
        scratch_shapes=[
            pltpu.VMEM(depth.shape, f32),
            pltpu.VMEM(pos.shape, jnp.int32),
            pltpu.VMEM(obs.shape, f32),
            pltpu.VMEM(scale.shape, f32),
            pltpu.VMEM(pert.shape, f32),
            pltpu.VMEM((fields, members, rows, cols), f32),
            pltpu.VMEM((members, rows, cols), f32),
            pltpu.VMEM((4, 2, members, 1, cols), f32),
            pltpu.VMEM((4, 2, members, 1, cols), f32),
            pltpu.VMEM((cols, n_obs), bf16),
            pltpu.VMEM((3 * members * rows, 512), bf16),
            pltpu.VMEM((nm, PAD, n_obs), f32),
            pltpu.VMEM((nm, PAD, n_obs), f32),
            pltpu.VMEM((gz, np_ // 2, 2 * np_), f32),
            pltpu.VMEM((gy, np_ // 2, 2 * np_), f32),
            pltpu.VMEM((2, np_ // 2, 2 * np_), f32),
            pltpu.VMEM((fields, nm, members, rows, cols // nm), f32),
            pltpu.VMEM((fields, nm, members, rows, cols // nm), f32),
            pltpu.VMEM((cells, np_), bf16),
            dma((fields,)),
            dma((5,)),
            dma((4, 2, members)),
            dma((4, 2, members)),
            dma((nm,)),
            dma((nm,)),
            dma((nm,)),
            dma((nm,)),
            dma((gz,)),
            dma((gz,)),
            dma((gy,)),
            dma((gy,)),
            dma,
            dma,
            dma((fields, nm)),
            dma((fields, nm)),
            dma((fields, nm)),
            dma((fields, nm)),
        ],
        compiler_params=pltpu.CompilerParams(
            collective_id=0, has_side_effects=True, vmem_limit_bytes=64 * 1024 * 1024 - 65536
        ),
        name="smoother",
    )(ens, depth, pos, obs, scale, pert, infl)


def solution(mesh):
    in_specs = (
        P("mem", None, "band", None),
        P("band", None),
        P("band", None),
        P("band", None),
        P("band", None),
        P("mem", "band", None),
        P(),
    )
    out_specs = P("mem", None, "band", None)
    return jax.shard_map(body, mesh=mesh, in_specs=in_specs, out_specs=out_specs, check_vma=False)
```

```python
import functools
import math

import jax
import jax.numpy as jnp
from jax import lax
from jax.experimental import pallas as pl
from jax.experimental.pallas import tpu as pltpu
from jax.sharding import PartitionSpec as P

MESH = pl.DeviceIdType.MESH
HIGHEST = lax.Precision.HIGHEST

coriolis_base = 0.15
coriolis_slope = 0.3
PAD = 8


def rows_of(shape):
    return lax.broadcasted_iota(jnp.int32, shape, 0)


def lanes_of(shape):
    return lax.broadcasted_iota(jnp.int32, shape, 1)


def east(q):
    n = q.shape[1]
    return pltpu.roll(q, n - 1, 1) - pltpu.roll(q, 1, 1)


def north(q, above, below):
    n = q.shape[0]
    row = rows_of(q.shape)
    after = jnp.where(row == n - 1, below, pltpu.roll(q, n - 1, 0))
    before = jnp.where(row == 0, above, pltpu.roll(q, 1, 0))
    return after - before


def nt(a, b, precision=None):
    return lax.dot_general(
        a, b, (((1,), (1,)), ((), ())), precision=precision, preferred_element_type=jnp.float32
    )


def kernel(
    nm, nb, gz,
    ens, depth_in, pos_in, obs_in, scale_in, pert_in, infl,
    out,
    depth, pos, obs, scale, pert,
    st, dv, hs, hr, onehot, hb, noise, pi, zb, yb, sb, xb, mb, spread_rows,
    load_sem, small_sem, hs_sem, hr_sem, ns_sem, nr_sem, as_sem, ar_sem, zs_sem, zr_sem, ys_sem, yr_sem,
    ss_sem, sr_sem, fs_sem, fr_sem, bs_sem, br_sem,
):
    _, members, rows, cols = st.shape
    n_obs = onehot.shape[1]
    width = cols // nm
    np_ = nm * PAD
    total = nm * members
    cells = total * rows
    gy = nb // gz
    norm = math.sqrt(total - 1)
    H, U, V = 0, 1, 2
    me, b = lax.axis_index("mem"), lax.axis_index("band")
    z, y = lax.rem(b, gz), lax.div(b, gz)
    mates = [lax.rem(me + s, nm) for s in range(1, nm)]

    small = [
        pltpu.make_async_copy(source, target, small_sem.at[k])
        for k, (source, target) in enumerate(
            [(depth_in, depth), (pos_in, pos), (obs_in, obs), (scale_in, scale), (pert_in, pert)]
        )
    ]
    load = [pltpu.make_async_copy(ens.at[:, f], st.at[f], load_sem.at[f]) for f in range(3)]
    small[0].start()
    load[V].start()
    small[4].start()
    load[U].start()
    load[H].start()
    for copy in small[1:4]:
        copy.start()

    barrier = pltpu.get_barrier_semaphore()

    def greet(where):
        pl.semaphore_signal(barrier, 1, device_id=where, device_id_type=MESH)

    for peer in mates:
        greet({"mem": peer})
    for s in range(1, gz):
        greet({"band": y * gz + lax.rem(z + s, gz)})
    for s in range(1, gy):
        greet({"band": lax.rem(y + s, gy) * gz + z})
    far_above = jnp.logical_and(z == 0, y > 0)
    far_below = jnp.logical_and(z == gz - 1, y < gy - 1)

    @pl.when(far_above)
    def _():
        greet({"band": b - 1})

    @pl.when(far_below)
    def _():
        greet({"band": b + 1})

    @pl.when(b == 0)
    def _():
        hr[:, 0] = jnp.zeros_like(hr[:, 0])

    @pl.when(b == nb - 1)
    def _():
        hr[:, 1] = jnp.zeros_like(hr[:, 1])

    def turn(lanes):
        row = (rows_of((rows, lanes)) + b * rows).astype(jnp.float32)
        return coriolis_base + coriolis_slope * (row + 0.5) / (nb * rows)

    def halo(t, side, m):
        return pltpu.make_async_remote_copy(
            src_ref=hs.at[t, side, m],
            dst_ref=hr.at[t, 1 - side, m],
            send_sem=hs_sem.at[t, side, m],
            recv_sem=hr_sem.at[t, 1 - side, m],
            device_id={"band": jnp.where(b > 0, b - 1, 0) if side == 0 else jnp.where(b < nb - 1, b + 1, b)},
            device_id_type=MESH,
        )

    def edges(t, m, q):
        hs[t, 0, m] = q[0:1]
        hs[t, 1, m] = q[rows - 1 : rows]

        @pl.when(b > 0)
        def _():
            halo(t, 0, m).start()

        @pl.when(b < nb - 1)
        def _():
            halo(t, 1, m).start()

    def arrive(t, m):
        @pl.when(b > 0)
        def _():
            halo(t, 1, m).wait_recv()

        @pl.when(b < nb - 1)
        def _():
            halo(t, 0, m).wait_recv()

    def tell(buf, send, recv, peer, src):
        return pltpu.make_async_remote_copy(
            src_ref=buf.at[src], dst_ref=buf.at[src], send_sem=send.at[peer],
            recv_sem=recv.at[src], device_id={"mem": peer}, device_id_type=MESH,
        )

    def share(buf, send, recv, slot, other, peer):
        return pltpu.make_async_remote_copy(
            src_ref=buf.at[slot], dst_ref=buf.at[slot], send_sem=send.at[other],
            recv_sem=recv.at[slot], device_id={"band": peer}, device_id_type=MESH,
        )

    def columns(peer):
        return pl.ds(pl.multiple_of(peer * width, width), width)

    def forth(f, peer, src):
        return pltpu.make_async_remote_copy(
            src_ref=st.at[f, :, :, columns(peer)], dst_ref=xb.at[f, src], send_sem=fs_sem.at[f, peer],
            recv_sem=fr_sem.at[f, src], device_id={"mem": peer}, device_id_type=MESH,
        )

    def forth_one(f, m, peer):
        return pltpu.make_async_remote_copy(
            src_ref=st.at[f, m, :, columns(peer)], dst_ref=xb.at[f, me, m], send_sem=fs_sem.at[f, peer],
            recv_sem=fr_sem.at[f, me], device_id={"mem": peer}, device_id_type=MESH,
        )

    def back(f, peer, src):
        return pltpu.make_async_remote_copy(
            src_ref=mb.at[f, peer], dst_ref=out.at[:, f, :, columns(src)], send_sem=bs_sem.at[f, peer],
            recv_sem=br_sem.at[f, src], device_id={"mem": peer}, device_id_type=MESH,
        )

    pl.semaphore_wait(
        barrier,
        nm - 1 + gz - 1 + gy - 1 + jnp.where(far_above, 1, 0) + jnp.where(far_below, 1, 0),
    )

    small[0].wait()
    load[V].wait()

    @pl.loop(0, members)
    def _(m):
        flux = depth[...] * st[V, m]
        dv[m] = flux
        edges(0, m, flux)

    def flat(x):
        return jnp.concatenate([x[q : q + 1, :] for q in range(x.shape[0])], axis=1)

    small[4].wait()
    slot = rows_of((PAD, n_obs))
    own_noise = jnp.zeros((PAD, n_obs), jnp.float32)
    for m in range(members):
        own_noise = jnp.where(slot == m, flat(pert[m]), own_noise)
    noise[me] = own_noise
    for peer in mates:
        tell(noise, ns_sem, nr_sem, peer, me).start()

    load[U].wait()
    load[H].wait()

    @pl.loop(0, members)
    def _(m):
        st[H, m] = st[H, m] - 0.25 * east(depth[...] * st[U, m])

    @pl.loop(0, members)
    def _(m):
        arrive(0, m)
        h = st[H, m] - 0.25 * north(dv[m], hr[0, 0, m], hr[0, 1, m])
        st[H, m] = h
        edges(1, m, h)
        st[U, m] = st[U, m] - 0.25 * east(h) + turn(cols) * st[V, m]
        for peer in mates:
            forth_one(U, m, peer).start()

    for copy in small[1:4]:
        copy.wait()

    local = flat(pos[...]) - b * (rows * cols)
    obs_row = lax.shift_right_logical(local, int(math.log2(cols)))
    obs_col = jnp.bitwise_and(local, cols - 1)
    step = 256

    @pl.loop(0, cols // step)
    def _(k):
        col = rows_of((step, n_obs)) + k * step
        onehot[pl.ds(pl.multiple_of(k * step, step), step), :] = jnp.where(
            col == obs_col, 1.0, 0.0
        ).astype(jnp.bfloat16)

    @pl.loop(0, members)
    def _(m):
        arrive(1, m)
        v = st[V, m] - 0.25 * north(st[H, m], hr[1, 0, m], hr[1, 1, m]) - turn(cols) * st[U, m]
        st[V, m] = v
        flux = depth[...] * v
        dv[m] = flux
        edges(2, m, flux)

    @pl.loop(0, members)
    def _(m):
        h = st[H, m] - 0.25 * east(depth[...] * st[U, m])
        arrive(2, m)
        st[H, m] = h - 0.25 * north(dv[m], hr[2, 0, m], hr[2, 1, m])

    tall = members * rows
    kstep = 512

    def pick(k, acc):
        at = pl.ds(pl.multiple_of(k * kstep, kstep), kstep)
        h = st[H, :, :, at].reshape(tall, kstep)
        hi = h.astype(jnp.bfloat16)
        rest = h - hi.astype(jnp.float32)
        mid = rest.astype(jnp.bfloat16)
        low = (rest - mid.astype(jnp.float32)).astype(jnp.bfloat16)
        hb[0:tall] = hi
        hb[tall : 2 * tall] = mid
        hb[2 * tall : 3 * tall] = low
        return acc + jnp.dot(hb[...], onehot[at, :], preferred_element_type=jnp.float32)

    picked = lax.fori_loop(0, cols // kstep, pick, jnp.zeros((3 * tall, n_obs), jnp.float32))
    picked = picked[0:tall] + (picked[tall : 2 * tall] + picked[2 * tall : 3 * tall])
    here = rows_of((rows, n_obs)) == obs_row
    own = jnp.zeros((PAD, n_obs), jnp.float32)
    for m in range(members):
        mine = jnp.where(here, picked[m * rows : (m + 1) * rows], 0.0)
        own = jnp.where(slot == m, jnp.sum(mine, axis=0, keepdims=True), own)
    pi[me] = own
    for peer in mates:
        tell(pi, as_sem, ar_sem, peer, me).start()
    for f in range(3):
        xb[f, me] = st[f, :, :, columns(me)]

    j = lax.shift_right_logical(rows_of((cells, np_)), int(math.log2(rows)))
    padded = j
    for k in range(1, nm):
        padded = padded + jnp.where(j >= k * members, PAD - members, 0)
    spread_rows[...] = jnp.where(lanes_of((cells, np_)) == padded, 1.0, 0.0).astype(jnp.bfloat16)

    err = flat(scale[...])
    factor = jnp.full((1, n_obs), infl[0], jnp.float32)
    known = flat(obs[...])
    weight = jnp.sqrt(factor) * err
    for peer in mates:
        tell(noise, ns_sem, nr_sem, peer, peer).wait_recv()
    aimed = known + weight * noise[...].reshape(np_, n_obs)
    for peer in mates:
        tell(pi, as_sem, ar_sem, peer, peer).wait_recv()
    predicted = pi[...].reshape(np_, n_obs)
    centre = jnp.sum(predicted, axis=0, keepdims=True) * (1.0 / total)
    inside = jnp.bitwise_and(rows_of((np_, n_obs)), PAD - 1) < members
    unit = err * norm
    spread = jnp.where(inside, (predicted - centre) / unit, 0.0)
    innovation = jnp.where(inside, (aimed - predicted) / err, 0.0)
    half = nm // 2
    core = lax.rem(me, 2)
    mine = pi[pl.ds(core * half, half)].reshape(half * PAD, n_obs)
    own_spread = jnp.where(inside[0 : half * PAD], (mine - centre) / unit, 0.0)
    zb[z] = nt(own_spread, jnp.concatenate([spread, innovation], axis=0), HIGHEST)
    others = [lax.rem(z + s, gz) for s in range(1, gz)]
    for other in others:
        share(zb, zs_sem, zr_sem, z, other, y * gz + other).start()
    for peer in mates:
        forth(V, peer, me).start()
    for peer in mates:
        forth(H, peer, me).start()
    for other in others:
        share(zb, zs_sem, zr_sem, other, other, y * gz + other).wait_recv()
    yb[y] = jnp.sum(zb[...], axis=0)
    layers = [lax.rem(y + s, gy) for s in range(1, gy)]
    for other in layers:
        share(yb, ys_sem, yr_sem, y, other, other * gz + z).start()
    for other in layers:
        share(yb, ys_sem, yr_sem, other, other, other * gz + z).wait_recv()
    sb[core] = jnp.sum(yb[...], axis=0)
    swap = pltpu.make_async_remote_copy(
        src_ref=sb.at[core], dst_ref=sb.at[core], send_sem=ss_sem, recv_sem=sr_sem,
        device_id={"mem": me + 1 - 2 * core}, device_id_type=MESH,
    )
    swap.start()
    swap.wait()

    shape = (PAD, 2 * np_)
    sub, lane = rows_of(shape), lanes_of(shape)
    blocks = [
        sb[k // half, (k % half) * PAD : (k % half + 1) * PAD]
        + jnp.where(sub + k * PAD == lane, infl[0], 0.0)
        for k in range(nm)
    ]
    for k in range(total):
        home, r = divmod(k, members)
        p = home * PAD + r
        line = blocks[home][r : r + 1]
        line = line / line[:, p : p + 1]
        new = [x - x[:, p : p + 1] * line for x in blocks]
        new[home] = jnp.where(sub == r, line, new[home])
        blocks = new
    weights = jnp.concatenate([x[:, np_:] for x in blocks], axis=0)
    square = (np_, np_)
    mean = jnp.sum(weights, axis=0, keepdims=True) * (1.0 / total)
    transform = jnp.where(rows_of(square) == lanes_of(square), 1.0, 0.0) + (weights - mean) * (1.0 / norm)

    alike = jnp.bitwise_and(rows_of((cells, cells)), rows - 1) == jnp.bitwise_and(
        lanes_of((cells, cells)), rows - 1
    )

    def widen(t):
        grown = nt(spread_rows[...], t).astype(jnp.bfloat16)
        return jnp.where(alike, nt(grown, spread_rows[...]), 0.0).astype(jnp.bfloat16)

    hi = transform.astype(jnp.bfloat16)
    mix_hi = widen(hi)
    mix_lo = widen((transform - hi.astype(jnp.float32)).astype(jnp.bfloat16))

    for f in (U, H, V):
        for peer in mates:
            forth(f, peer, peer).wait_recv()
        x = xb[f].reshape(cells, width)
        x_hi = x.astype(jnp.bfloat16)
        x_lo = (x - x_hi.astype(jnp.float32)).astype(jnp.bfloat16)
        mixed = jnp.dot(mix_hi, x_hi, preferred_element_type=jnp.float32) + (
            jnp.dot(mix_hi, x_lo, preferred_element_type=jnp.float32)
            + jnp.dot(mix_lo, x_hi, preferred_element_type=jnp.float32)
        )
        mb[f] = mixed.reshape(nm, members, rows, width)
        if f == V:
            for peer in mates:
                back(H, peer, me).wait_send()
        for peer in mates:
            back(f, peer, me).start()
        out[:, f, :, columns(me)] = mb[f, me]

    for peer in mates:
        back(H, peer, peer).wait_recv()

    @pl.loop(0, members)
    def _(m):
        edges(3, m, out[m, H])

    for peer in mates:
        back(U, peer, peer).wait_recv()

    @pl.loop(0, members)
    def _(m):
        out[m, U] = out[m, U] - 0.25 * east(out[m, H])

    @pl.loop(0, members)
    def _(m):
        arrive(3, m)
        dv[m] = 0.25 * north(out[m, H], hr[3, 0, m], hr[3, 1, m])

    def finish(src):
        at = columns(src)
        f = turn(width)
        for m in range(members):
            v = out[m, V, :, at]
            u = out[m, U, :, at] + f * v
            out[m, U, :, at] = u
            out[m, V, :, at] = v - dv[m, :, at] - f * u

    finish(me)

    @pl.loop(1, nm)
    def _(s):
        peer = lax.rem(me + s, nm)
        back(V, peer, peer).wait_recv()
        finish(peer)

    @pl.loop(0, members)
    def _(m):
        for t in range(4):

            @pl.when(b > 0)
            def _():
                halo(t, 0, m).wait_send()

            @pl.when(b < nb - 1)
            def _():
                halo(t, 1, m).wait_send()

    for peer in mates:
        tell(noise, ns_sem, nr_sem, peer, me).wait_send()
        tell(pi, as_sem, ar_sem, peer, me).wait_send()
    for other in others:
        share(zb, zs_sem, zr_sem, z, other, y * gz + other).wait_send()
    for other in layers:
        share(yb, ys_sem, yr_sem, y, other, other * gz + z).wait_send()
    for peer in mates:
        for f in range(3):
            forth(f, peer, me).wait_send()
        back(U, peer, me).wait_send()
        back(V, peer, me).wait_send()


def body(ens, depth, pos, obs, scale, pert, infl):
    nm, nb = lax.axis_size("mem"), lax.axis_size("band")
    gz = 8 if nb >= 16 else 2
    gy = nb // gz
    members, fields, rows, cols = ens.shape
    n_obs = pos.size
    np_ = nm * PAD
    cells = nm * members * rows
    f32, bf16 = jnp.float32, jnp.bfloat16
    dma = pltpu.SemaphoreType.DMA
    vmem = pl.BlockSpec(memory_space=pltpu.VMEM)
    return pl.pallas_call(
        functools.partial(kernel, nm, nb, gz),
        out_shape=jax.ShapeDtypeStruct(ens.shape, f32),
        in_specs=[pl.BlockSpec(memory_space=pltpu.HBM)] * 6 + [pl.BlockSpec(memory_space=pltpu.SMEM)],
        out_specs=vmem,
        scratch_shapes=[
            pltpu.VMEM(depth.shape, f32),
            pltpu.VMEM(pos.shape, jnp.int32),
            pltpu.VMEM(obs.shape, f32),
            pltpu.VMEM(scale.shape, f32),
            pltpu.VMEM(pert.shape, f32),
            pltpu.VMEM((fields, members, rows, cols), f32),
            pltpu.VMEM((members, rows, cols), f32),
            pltpu.VMEM((4, 2, members, 1, cols), f32),
            pltpu.VMEM((4, 2, members, 1, cols), f32),
            pltpu.VMEM((cols, n_obs), bf16),
            pltpu.VMEM((3 * members * rows, 512), bf16),
            pltpu.VMEM((nm, PAD, n_obs), f32),
            pltpu.VMEM((nm, PAD, n_obs), f32),
            pltpu.VMEM((gz, np_ // 2, 2 * np_), f32),
            pltpu.VMEM((gy, np_ // 2, 2 * np_), f32),
            pltpu.VMEM((2, np_ // 2, 2 * np_), f32),
            pltpu.VMEM((fields, nm, members, rows, cols // nm), f32),
            pltpu.VMEM((fields, nm, members, rows, cols // nm), f32),
            pltpu.VMEM((cells, np_), bf16),
            dma((fields,)),
            dma((5,)),
            dma((4, 2, members)),
            dma((4, 2, members)),
            dma((nm,)),
            dma((nm,)),
            dma((nm,)),
            dma((nm,)),
            dma((gz,)),
            dma((gz,)),
            dma((gy,)),
            dma((gy,)),
            dma,
            dma,
            dma((fields, nm)),
            dma((fields, nm)),
            dma((fields, nm)),
            dma((fields, nm)),
        ],
        compiler_params=pltpu.CompilerParams(
            collective_id=0, has_side_effects=True, vmem_limit_bytes=48 * 1024 * 1024
        ),
        name="smoother",
    )(*[pltpu.with_memory_space_constraint(x, pltpu.HBM) for x in (ens, depth, pos, obs, scale, pert)], infl)


def solution(mesh):
    in_specs = (
        P("mem", None, "band", None),
        P("band", None),
        P("band", None),
        P("band", None),
        P("band", None),
        P("mem", "band", None),
        P(),
    )
    out_specs = P("mem", None, "band", None)
    return jax.shard_map(body, mesh=mesh, in_specs=in_specs, out_specs=out_specs, check_vma=False)
```

```python
import functools
import math

import jax
import jax.numpy as jnp
from jax import lax
from jax.experimental import pallas as pl
from jax.experimental.pallas import tpu as pltpu
from jax.sharding import PartitionSpec as P

MESH = pl.DeviceIdType.MESH
HIGHEST = lax.Precision.HIGHEST

coriolis_base = 0.15
coriolis_slope = 0.3
PAD = 8


def rows_of(shape):
    return lax.broadcasted_iota(jnp.int32, shape, 0)


def lanes_of(shape):
    return lax.broadcasted_iota(jnp.int32, shape, 1)


def east(q):
    n = q.shape[1]
    return pltpu.roll(q, n - 1, 1) - pltpu.roll(q, 1, 1)


def north(q, above, below):
    n = q.shape[0]
    row = rows_of(q.shape)
    after = jnp.where(row == n - 1, below, pltpu.roll(q, n - 1, 0))
    before = jnp.where(row == 0, above, pltpu.roll(q, 1, 0))
    return after - before


def nt(a, b, precision=None):
    return lax.dot_general(
        a, b, (((1,), (1,)), ((), ())), precision=precision, preferred_element_type=jnp.float32
    )


def kernel(
    nm, nb, gz,
    ens, depth_in, pos_in, obs_in, scale_in, pert_in, infl,
    out,
    depth, pos, obs, scale, pert,
    st, dv, hs, hr, onehot, hb, noise, pi, zb, yb, sb, xb, mb, spread_rows,
    load_sem, small_sem, hs_sem, hr_sem, ns_sem, nr_sem, as_sem, ar_sem, zs_sem, zr_sem, ys_sem, yr_sem,
    ss_sem, sr_sem, fs_sem, fr_sem, bs_sem, br_sem,
):
    _, members, rows, cols = st.shape
    n_obs = onehot.shape[1]
    width = cols // nm
    np_ = nm * PAD
    total = nm * members
    cells = total * rows
    gy = nb // gz
    norm = math.sqrt(total - 1)
    H, U, V = 0, 1, 2
    me, b = lax.axis_index("mem"), lax.axis_index("band")
    z, y = lax.rem(b, gz), lax.div(b, gz)
    mates = [lax.rem(me + s, nm) for s in range(1, nm)]

    small = [
        pltpu.make_async_copy(source, target, small_sem.at[k])
        for k, (source, target) in enumerate(
            [(depth_in, depth), (pos_in, pos), (obs_in, obs), (scale_in, scale), (pert_in, pert)]
        )
    ]
    load = [pltpu.make_async_copy(ens.at[:, f], st.at[f], load_sem.at[f]) for f in range(3)]
    small[0].start()
    load[V].start()
    small[4].start()
    load[U].start()
    load[H].start()
    for copy in small[1:4]:
        copy.start()

    barrier = pltpu.get_barrier_semaphore()

    def greet(where):
        pl.semaphore_signal(barrier, 1, device_id=where, device_id_type=MESH)

    for peer in mates:
        greet({"mem": peer})
    for s in range(1, gz):
        greet({"band": y * gz + lax.rem(z + s, gz)})
    for s in range(1, gy):
        greet({"band": lax.rem(y + s, gy) * gz + z})
    far_above = jnp.logical_and(z == 0, y > 0)
    far_below = jnp.logical_and(z == gz - 1, y < gy - 1)

    @pl.when(far_above)
    def _():
        greet({"band": b - 1})

    @pl.when(far_below)
    def _():
        greet({"band": b + 1})

    @pl.when(b == 0)
    def _():
        hr[:, 0] = jnp.zeros_like(hr[:, 0])

    @pl.when(b == nb - 1)
    def _():
        hr[:, 1] = jnp.zeros_like(hr[:, 1])

    def turn(lanes):
        row = (rows_of((rows, lanes)) + b * rows).astype(jnp.float32)
        return coriolis_base + coriolis_slope * (row + 0.5) / (nb * rows)

    def halo(t, side, m):
        return pltpu.make_async_remote_copy(
            src_ref=hs.at[t, side, m],
            dst_ref=hr.at[t, 1 - side, m],
            send_sem=hs_sem.at[t, side, m],
            recv_sem=hr_sem.at[t, 1 - side, m],
            device_id={"band": jnp.where(b > 0, b - 1, 0) if side == 0 else jnp.where(b < nb - 1, b + 1, b)},
            device_id_type=MESH,
        )

    def edges(t, m, q):
        hs[t, 0, m] = q[0:1]
        hs[t, 1, m] = q[rows - 1 : rows]

        @pl.when(b > 0)
        def _():
            halo(t, 0, m).start()

        @pl.when(b < nb - 1)
        def _():
            halo(t, 1, m).start()

    def arrive(t, m):
        @pl.when(b > 0)
        def _():
            halo(t, 1, m).wait_recv()

        @pl.when(b < nb - 1)
        def _():
            halo(t, 0, m).wait_recv()

    def tell(buf, send, recv, peer, src):
        return pltpu.make_async_remote_copy(
            src_ref=buf.at[src], dst_ref=buf.at[src], send_sem=send.at[peer],
            recv_sem=recv.at[src], device_id={"mem": peer}, device_id_type=MESH,
        )

    def share(buf, send, recv, slot, other, peer):
        return pltpu.make_async_remote_copy(
            src_ref=buf.at[slot], dst_ref=buf.at[slot], send_sem=send.at[other],
            recv_sem=recv.at[slot], device_id={"band": peer}, device_id_type=MESH,
        )

    def columns(peer):
        return pl.ds(pl.multiple_of(peer * width, width), width)

    def forth(f, peer, src):
        return pltpu.make_async_remote_copy(
            src_ref=st.at[f, :, :, columns(peer)], dst_ref=xb.at[f, src], send_sem=fs_sem.at[f, peer],
            recv_sem=fr_sem.at[f, src], device_id={"mem": peer}, device_id_type=MESH,
        )

    def forth_one(f, m, peer):
        return pltpu.make_async_remote_copy(
            src_ref=st.at[f, m, :, columns(peer)], dst_ref=xb.at[f, me, m], send_sem=fs_sem.at[f, peer],
            recv_sem=fr_sem.at[f, me], device_id={"mem": peer}, device_id_type=MESH,
        )

    def back(f, peer, src):
        return pltpu.make_async_remote_copy(
            src_ref=mb.at[f, peer], dst_ref=out.at[:, f, :, columns(src)], send_sem=bs_sem.at[f, peer],
            recv_sem=br_sem.at[f, src], device_id={"mem": peer}, device_id_type=MESH,
        )

    pl.semaphore_wait(
        barrier,
        nm - 1 + gz - 1 + gy - 1 + jnp.where(far_above, 1, 0) + jnp.where(far_below, 1, 0),
    )

    small[0].wait()
    load[V].wait()

    @pl.loop(0, members)
    def _(m):
        flux = depth[...] * st[V, m]
        dv[m] = flux
        edges(0, m, flux)

    def flat(x):
        return jnp.concatenate([x[q : q + 1, :] for q in range(x.shape[0])], axis=1)

    small[4].wait()
    slot = rows_of((PAD, n_obs))
    own_noise = jnp.zeros((PAD, n_obs), jnp.float32)
    for m in range(members):
        own_noise = jnp.where(slot == m, flat(pert[m]), own_noise)
    noise[me] = own_noise
    for peer in mates:
        tell(noise, ns_sem, nr_sem, peer, me).start()

    load[U].wait()
    load[H].wait()

    @pl.loop(0, members)
    def _(m):
        st[H, m] = st[H, m] - 0.25 * east(depth[...] * st[U, m])

    @pl.loop(0, members)
    def _(m):
        arrive(0, m)
        h = st[H, m] - 0.25 * north(dv[m], hr[0, 0, m], hr[0, 1, m])
        st[H, m] = h
        edges(1, m, h)
        st[U, m] = st[U, m] - 0.25 * east(h) + turn(cols) * st[V, m]
        for peer in mates:
            forth_one(U, m, peer).start()

    for copy in small[1:4]:
        copy.wait()

    local = flat(pos[...]) - b * (rows * cols)
    obs_row = lax.shift_right_logical(local, int(math.log2(cols)))
    obs_col = jnp.bitwise_and(local, cols - 1)
    step = 256

    @pl.loop(0, cols // step)
    def _(k):
        col = rows_of((step, n_obs)) + k * step
        onehot[pl.ds(pl.multiple_of(k * step, step), step), :] = jnp.where(
            col == obs_col, 1.0, 0.0
        ).astype(jnp.bfloat16)

    @pl.loop(0, members)
    def _(m):
        arrive(1, m)
        v = st[V, m] - 0.25 * north(st[H, m], hr[1, 0, m], hr[1, 1, m]) - turn(cols) * st[U, m]
        st[V, m] = v
        flux = depth[...] * v
        dv[m] = flux
        edges(2, m, flux)

    @pl.loop(0, members)
    def _(m):
        h = st[H, m] - 0.25 * east(depth[...] * st[U, m])
        arrive(2, m)
        st[H, m] = h - 0.25 * north(dv[m], hr[2, 0, m], hr[2, 1, m])

    tall = members * rows
    kstep = 512

    def pick(k, acc):
        at = pl.ds(pl.multiple_of(k * kstep, kstep), kstep)
        h = st[H, :, :, at].reshape(tall, kstep)
        hi = h.astype(jnp.bfloat16)
        rest = h - hi.astype(jnp.float32)
        mid = rest.astype(jnp.bfloat16)
        low = (rest - mid.astype(jnp.float32)).astype(jnp.bfloat16)
        hb[0:tall] = hi
        hb[tall : 2 * tall] = mid
        hb[2 * tall : 3 * tall] = low
        return acc + jnp.dot(hb[...], onehot[at, :], preferred_element_type=jnp.float32)

    picked = lax.fori_loop(0, cols // kstep, pick, jnp.zeros((3 * tall, n_obs), jnp.float32))
    picked = picked[0:tall] + (picked[tall : 2 * tall] + picked[2 * tall : 3 * tall])
    here = rows_of((rows, n_obs)) == obs_row
    own = jnp.zeros((PAD, n_obs), jnp.float32)
    for m in range(members):
        mine = jnp.where(here, picked[m * rows : (m + 1) * rows], 0.0)
        own = jnp.where(slot == m, jnp.sum(mine, axis=0, keepdims=True), own)
    pi[me] = own
    for peer in mates:
        tell(pi, as_sem, ar_sem, peer, me).start()
    for f in range(3):
        xb[f, me] = st[f, :, :, columns(me)]

    j = lax.shift_right_logical(rows_of((cells, np_)), int(math.log2(rows)))
    padded = j
    for k in range(1, nm):
        padded = padded + jnp.where(j >= k * members, PAD - members, 0)
    spread_rows[...] = jnp.where(lanes_of((cells, np_)) == padded, 1.0, 0.0).astype(jnp.bfloat16)

    err = flat(scale[...])
    factor = jnp.full((1, n_obs), infl[0], jnp.float32)
    known = flat(obs[...])
    weight = jnp.sqrt(factor) * err
    for peer in mates:
        tell(noise, ns_sem, nr_sem, peer, peer).wait_recv()
    aimed = known + weight * noise[...].reshape(np_, n_obs)
    for peer in mates:
        tell(pi, as_sem, ar_sem, peer, peer).wait_recv()
    predicted = pi[...].reshape(np_, n_obs)
    centre = jnp.sum(predicted, axis=0, keepdims=True) * (1.0 / total)
    inside = jnp.bitwise_and(rows_of((np_, n_obs)), PAD - 1) < members
    unit = err * norm
    spread = jnp.where(inside, (predicted - centre) / unit, 0.0)
    innovation = jnp.where(inside, (aimed - predicted) / err, 0.0)
    half = nm // 2
    core = lax.rem(me, 2)
    mine = pi[pl.ds(core * half, half)].reshape(half * PAD, n_obs)
    own_spread = jnp.where(inside[0 : half * PAD], (mine - centre) / unit, 0.0)
    zb[z] = nt(own_spread, jnp.concatenate([spread, innovation], axis=0), HIGHEST)
    others = [lax.rem(z + s, gz) for s in range(1, gz)]
    for other in others:
        share(zb, zs_sem, zr_sem, z, other, y * gz + other).start()
    for peer in mates:
        forth(V, peer, me).start()
    for peer in mates:
        forth(H, peer, me).start()
    for other in others:
        share(zb, zs_sem, zr_sem, other, other, y * gz + other).wait_recv()
    yb[y] = jnp.sum(zb[...], axis=0)
    layers = [lax.rem(y + s, gy) for s in range(1, gy)]
    for other in layers:
        share(yb, ys_sem, yr_sem, y, other, other * gz + z).start()
    for other in layers:
        share(yb, ys_sem, yr_sem, other, other, other * gz + z).wait_recv()
    sb[core] = jnp.sum(yb[...], axis=0)
    swap = pltpu.make_async_remote_copy(
        src_ref=sb.at[core], dst_ref=sb.at[core], send_sem=ss_sem, recv_sem=sr_sem,
        device_id={"mem": me + 1 - 2 * core}, device_id_type=MESH,
    )
    swap.start()
    swap.wait()

    shape = (PAD, 2 * np_)
    sub, lane = rows_of(shape), lanes_of(shape)
    blocks = [
        sb[k // half, (k % half) * PAD : (k % half + 1) * PAD]
        + jnp.where(sub + k * PAD == lane, infl[0], 0.0)
        for k in range(nm)
    ]
    for k in range(0, total, 2):
        home, r = divmod(k, members)
        p = home * PAD + r
        one, two = blocks[home][r : r + 1], blocks[home][r + 1 : r + 2]
        def lanes(x, at):
            return jnp.broadcast_to(x[:, at : at + 1], x.shape)

        a, c, d, e = lanes(one, p), lanes(one, p + 1), lanes(two, p), lanes(two, p + 1)
        scale_ = 1.0 / (a * e - c * d)
        first = (e * scale_) * one - (c * scale_) * two
        second = (a * scale_) * two - (d * scale_) * one
        new = [x - x[:, p : p + 1] * first - x[:, p + 1 : p + 2] * second for x in blocks]
        new[home] = jnp.where(sub == r, first, jnp.where(sub == r + 1, second, new[home]))
        blocks = new
    weights = jnp.concatenate([x[:, np_:] for x in blocks], axis=0)
    square = (np_, np_)
    mean = jnp.sum(weights, axis=0, keepdims=True) * (1.0 / total)
    transform = jnp.where(rows_of(square) == lanes_of(square), 1.0, 0.0) + (weights - mean) * (1.0 / norm)

    alike = jnp.bitwise_and(rows_of((cells, cells)), rows - 1) == jnp.bitwise_and(
        lanes_of((cells, cells)), rows - 1
    )

    def widen(t):
        grown = nt(spread_rows[...], t).astype(jnp.bfloat16)
        return jnp.where(alike, nt(grown, spread_rows[...]), 0.0).astype(jnp.bfloat16)

    hi = transform.astype(jnp.bfloat16)
    mix_hi = widen(hi)
    mix_lo = widen((transform - hi.astype(jnp.float32)).astype(jnp.bfloat16))

    for f in (U, H, V):
        for peer in mates:
            forth(f, peer, peer).wait_recv()
        x = xb[f].reshape(cells, width)
        x_hi = x.astype(jnp.bfloat16)
        x_lo = (x - x_hi.astype(jnp.float32)).astype(jnp.bfloat16)
        mixed = jnp.dot(mix_hi, x_hi, preferred_element_type=jnp.float32) + (
            jnp.dot(mix_hi, x_lo, preferred_element_type=jnp.float32)
            + jnp.dot(mix_lo, x_hi, preferred_element_type=jnp.float32)
        )
        mb[f] = mixed.reshape(nm, members, rows, width)
        if f == V:
            for peer in mates:
                back(H, peer, me).wait_send()
        for peer in mates:
            back(f, peer, me).start()
        out[:, f, :, columns(me)] = mb[f, me]

    for peer in mates:
        back(H, peer, peer).wait_recv()

    @pl.loop(0, members)
    def _(m):
        edges(3, m, out[m, H])

    for peer in mates:
        back(U, peer, peer).wait_recv()

    @pl.loop(0, members)
    def _(m):
        out[m, U] = out[m, U] - 0.25 * east(out[m, H])

    @pl.loop(0, members)
    def _(m):
        arrive(3, m)
        dv[m] = 0.25 * north(out[m, H], hr[3, 0, m], hr[3, 1, m])

    def finish(src):
        at = columns(src)
        f = turn(width)
        for m in range(members):
            v = out[m, V, :, at]
            u = out[m, U, :, at] + f * v
            out[m, U, :, at] = u
            out[m, V, :, at] = v - dv[m, :, at] - f * u

    finish(me)

    @pl.loop(1, nm)
    def _(s):
        peer = lax.rem(me + s, nm)
        back(V, peer, peer).wait_recv()
        finish(peer)

    @pl.loop(0, members)
    def _(m):
        for t in range(4):

            @pl.when(b > 0)
            def _():
                halo(t, 0, m).wait_send()

            @pl.when(b < nb - 1)
            def _():
                halo(t, 1, m).wait_send()

    for peer in mates:
        tell(noise, ns_sem, nr_sem, peer, me).wait_send()
        tell(pi, as_sem, ar_sem, peer, me).wait_send()
    for other in others:
        share(zb, zs_sem, zr_sem, z, other, y * gz + other).wait_send()
    for other in layers:
        share(yb, ys_sem, yr_sem, y, other, other * gz + z).wait_send()
    for peer in mates:
        for f in range(3):
            forth(f, peer, me).wait_send()
        back(U, peer, me).wait_send()
        back(V, peer, me).wait_send()


def body(ens, depth, pos, obs, scale, pert, infl):
    nm, nb = lax.axis_size("mem"), lax.axis_size("band")
    gz = 8 if nb >= 16 else 2
    gy = nb // gz
    members, fields, rows, cols = ens.shape
    n_obs = pos.size
    np_ = nm * PAD
    cells = nm * members * rows
    f32, bf16 = jnp.float32, jnp.bfloat16
    dma = pltpu.SemaphoreType.DMA
    vmem = pl.BlockSpec(memory_space=pltpu.VMEM)
    return pl.pallas_call(
        functools.partial(kernel, nm, nb, gz),
        out_shape=jax.ShapeDtypeStruct(ens.shape, f32),
        in_specs=[pl.BlockSpec(memory_space=pltpu.HBM)] * 6 + [pl.BlockSpec(memory_space=pltpu.SMEM)],
        out_specs=vmem,
        scratch_shapes=[
            pltpu.VMEM(depth.shape, f32),
            pltpu.VMEM(pos.shape, jnp.int32),
            pltpu.VMEM(obs.shape, f32),
            pltpu.VMEM(scale.shape, f32),
            pltpu.VMEM(pert.shape, f32),
            pltpu.VMEM((fields, members, rows, cols), f32),
            pltpu.VMEM((members, rows, cols), f32),
            pltpu.VMEM((4, 2, members, 1, cols), f32),
            pltpu.VMEM((4, 2, members, 1, cols), f32),
            pltpu.VMEM((cols, n_obs), bf16),
            pltpu.VMEM((3 * members * rows, 512), bf16),
            pltpu.VMEM((nm, PAD, n_obs), f32),
            pltpu.VMEM((nm, PAD, n_obs), f32),
            pltpu.VMEM((gz, np_ // 2, 2 * np_), f32),
            pltpu.VMEM((gy, np_ // 2, 2 * np_), f32),
            pltpu.VMEM((2, np_ // 2, 2 * np_), f32),
            pltpu.VMEM((fields, nm, members, rows, cols // nm), f32),
            pltpu.VMEM((fields, nm, members, rows, cols // nm), f32),
            pltpu.VMEM((cells, np_), bf16),
            dma((fields,)),
            dma((5,)),
            dma((4, 2, members)),
            dma((4, 2, members)),
            dma((nm,)),
            dma((nm,)),
            dma((nm,)),
            dma((nm,)),
            dma((gz,)),
            dma((gz,)),
            dma((gy,)),
            dma((gy,)),
            dma,
            dma,
            dma((fields, nm)),
            dma((fields, nm)),
            dma((fields, nm)),
            dma((fields, nm)),
        ],
        compiler_params=pltpu.CompilerParams(
            collective_id=0, has_side_effects=True, vmem_limit_bytes=48 * 1024 * 1024
        ),
        name="smoother",
    )(*[pltpu.with_memory_space_constraint(x, pltpu.HBM) for x in (ens, depth, pos, obs, scale, pert)], infl)


def solution(mesh):
    in_specs = (
        P("mem", None, "band", None),
        P("band", None),
        P("band", None),
        P("band", None),
        P("band", None),
        P("mem", "band", None),
        P(),
    )
    out_specs = P("mem", None, "band", None)
    return jax.shard_map(body, mesh=mesh, in_specs=in_specs, out_specs=out_specs, check_vma=False)
```

```python
import functools
import math

import jax
import jax.numpy as jnp
from jax import lax
from jax.experimental import pallas as pl
from jax.experimental.pallas import tpu as pltpu
from jax.sharding import PartitionSpec as P

MESH = pl.DeviceIdType.MESH
HIGHEST = lax.Precision.HIGHEST

coriolis_base = 0.15
coriolis_slope = 0.3
PAD = 8


def rows_of(shape):
    return lax.broadcasted_iota(jnp.int32, shape, 0)


def lanes_of(shape):
    return lax.broadcasted_iota(jnp.int32, shape, 1)


def east(q):
    n = q.shape[1]
    return pltpu.roll(q, n - 1, 1) - pltpu.roll(q, 1, 1)


def north(q, above, below):
    n = q.shape[0]
    row = rows_of(q.shape)
    after = jnp.where(row == n - 1, below, pltpu.roll(q, n - 1, 0))
    before = jnp.where(row == 0, above, pltpu.roll(q, 1, 0))
    return after - before


def nt(a, b, precision=None):
    return lax.dot_general(
        a, b, (((1,), (1,)), ((), ())), precision=precision, preferred_element_type=jnp.float32
    )


def kernel(
    nm, nb, gz,
    ens, depth_in, pos_in, obs_in, scale_in, pert_in, infl,
    out,
    depth, pos, obs, scale, pert,
    st, dv, hs, hr, onehot, hb, noise, pi, zb, yb, sb, xb, mb, spread_rows,
    load_sem, small_sem, hs_sem, hr_sem, ns_sem, nr_sem, as_sem, ar_sem, zs_sem, zr_sem, ys_sem, yr_sem,
    ss_sem, sr_sem, fs_sem, fr_sem, bs_sem, br_sem,
):
    _, members, rows, cols = st.shape
    n_obs = onehot.shape[1]
    width = cols // nm
    np_ = nm * PAD
    total = nm * members
    cells = total * rows
    gy = nb // gz
    norm = math.sqrt(total - 1)
    H, U, V = 0, 1, 2
    me, b = lax.axis_index("mem"), lax.axis_index("band")
    z, y = lax.rem(b, gz), lax.div(b, gz)
    mates = [lax.rem(me + s, nm) for s in range(1, nm)]

    small = [
        pltpu.make_async_copy(source, target, small_sem.at[k])
        for k, (source, target) in enumerate(
            [(depth_in, depth), (pos_in, pos), (obs_in, obs), (scale_in, scale), (pert_in, pert)]
        )
    ]
    load = [pltpu.make_async_copy(ens.at[:, f], st.at[f], load_sem.at[f]) for f in range(3)]
    small[0].start()
    load[V].start()
    small[4].start()
    load[U].start()
    load[H].start()
    for copy in small[1:4]:
        copy.start()

    barrier = pltpu.get_barrier_semaphore()

    def greet(where):
        pl.semaphore_signal(barrier, 1, device_id=where, device_id_type=MESH)

    for peer in mates:
        greet({"mem": peer})
    for s in range(1, gz):
        greet({"band": y * gz + lax.rem(z + s, gz)})
    for s in range(1, gy):
        greet({"band": lax.rem(y + s, gy) * gz + z})
    far_above = jnp.logical_and(z == 0, y > 0)
    far_below = jnp.logical_and(z == gz - 1, y < gy - 1)

    @pl.when(far_above)
    def _():
        greet({"band": b - 1})

    @pl.when(far_below)
    def _():
        greet({"band": b + 1})

    @pl.when(b == 0)
    def _():
        hr[:, 0] = jnp.zeros_like(hr[:, 0])

    @pl.when(b == nb - 1)
    def _():
        hr[:, 1] = jnp.zeros_like(hr[:, 1])

    def turn(lanes):
        row = (rows_of((rows, lanes)) + b * rows).astype(jnp.float32)
        return coriolis_base + coriolis_slope * (row + 0.5) / (nb * rows)

    def halo(t, side, m):
        return pltpu.make_async_remote_copy(
            src_ref=hs.at[t, side, m],
            dst_ref=hr.at[t, 1 - side, m],
            send_sem=hs_sem.at[t, side, m],
            recv_sem=hr_sem.at[t, 1 - side, m],
            device_id={"band": jnp.where(b > 0, b - 1, 0) if side == 0 else jnp.where(b < nb - 1, b + 1, b)},
            device_id_type=MESH,
        )

    def edges(t, m, q):
        hs[t, 0, m] = q[0:1]
        hs[t, 1, m] = q[rows - 1 : rows]

        @pl.when(b > 0)
        def _():
            halo(t, 0, m).start()

        @pl.when(b < nb - 1)
        def _():
            halo(t, 1, m).start()

    def arrive(t, m):
        @pl.when(b > 0)
        def _():
            halo(t, 1, m).wait_recv()

        @pl.when(b < nb - 1)
        def _():
            halo(t, 0, m).wait_recv()

    def tell(buf, send, recv, peer, src):
        return pltpu.make_async_remote_copy(
            src_ref=buf.at[src], dst_ref=buf.at[src], send_sem=send.at[peer],
            recv_sem=recv.at[src], device_id={"mem": peer}, device_id_type=MESH,
        )

    def share(buf, send, recv, slot, other, peer):
        return pltpu.make_async_remote_copy(
            src_ref=buf.at[slot], dst_ref=buf.at[slot], send_sem=send.at[other],
            recv_sem=recv.at[slot], device_id={"band": peer}, device_id_type=MESH,
        )

    def columns(peer):
        return pl.ds(pl.multiple_of(peer * width, width), width)

    def forth(f, peer, src):
        return pltpu.make_async_remote_copy(
            src_ref=st.at[f, :, :, columns(peer)], dst_ref=xb.at[f, src], send_sem=fs_sem.at[f, peer],
            recv_sem=fr_sem.at[f, src], device_id={"mem": peer}, device_id_type=MESH,
        )

    def forth_one(f, m, peer):
        return pltpu.make_async_remote_copy(
            src_ref=st.at[f, m, :, columns(peer)], dst_ref=xb.at[f, me, m], send_sem=fs_sem.at[f, peer],
            recv_sem=fr_sem.at[f, me], device_id={"mem": peer}, device_id_type=MESH,
        )

    def back(f, peer, src):
        return pltpu.make_async_remote_copy(
            src_ref=mb.at[f, peer], dst_ref=out.at[:, f, :, columns(src)], send_sem=bs_sem.at[f, peer],
            recv_sem=br_sem.at[f, src], device_id={"mem": peer}, device_id_type=MESH,
        )

    pl.semaphore_wait(
        barrier,
        nm - 1 + gz - 1 + gy - 1 + jnp.where(far_above, 1, 0) + jnp.where(far_below, 1, 0),
    )

    small[0].wait()
    load[V].wait()

    @pl.loop(0, members)
    def _(m):
        flux = depth[...] * st[V, m]
        dv[m] = flux
        edges(0, m, flux)

    def flat(x):
        return jnp.concatenate([x[q : q + 1, :] for q in range(x.shape[0])], axis=1)

    small[4].wait()
    slot = rows_of((PAD, n_obs))
    own_noise = jnp.zeros((PAD, n_obs), jnp.float32)
    for m in range(members):
        own_noise = jnp.where(slot == m, flat(pert[m]), own_noise)
    noise[me] = own_noise
    for peer in mates:
        tell(noise, ns_sem, nr_sem, peer, me).start()

    load[U].wait()
    load[H].wait()

    @pl.loop(0, members)
    def _(m):
        st[H, m] = st[H, m] - 0.25 * east(depth[...] * st[U, m])

    @pl.loop(0, members)
    def _(m):
        arrive(0, m)
        h = st[H, m] - 0.25 * north(dv[m], hr[0, 0, m], hr[0, 1, m])
        st[H, m] = h
        edges(1, m, h)
        st[U, m] = st[U, m] - 0.25 * east(h) + turn(cols) * st[V, m]
        for peer in mates:
            forth_one(U, m, peer).start()

    for copy in small[1:4]:
        copy.wait()

    local = flat(pos[...]) - b * (rows * cols)
    obs_row = lax.shift_right_logical(local, int(math.log2(cols)))
    obs_col = jnp.bitwise_and(local, cols - 1)
    step = 256

    @pl.loop(0, cols // step)
    def _(k):
        col = rows_of((step, n_obs)) + k * step
        onehot[pl.ds(pl.multiple_of(k * step, step), step), :] = jnp.where(
            col == obs_col, 1.0, 0.0
        ).astype(jnp.bfloat16)

    @pl.loop(0, members)
    def _(m):
        arrive(1, m)
        v = st[V, m] - 0.25 * north(st[H, m], hr[1, 0, m], hr[1, 1, m]) - turn(cols) * st[U, m]
        st[V, m] = v
        flux = depth[...] * v
        dv[m] = flux
        edges(2, m, flux)

    @pl.loop(0, members)
    def _(m):
        h = st[H, m] - 0.25 * east(depth[...] * st[U, m])
        arrive(2, m)
        st[H, m] = h - 0.25 * north(dv[m], hr[2, 0, m], hr[2, 1, m])

    tall = members * rows
    kstep = cols // 2

    def pick(k, acc):
        at = pl.ds(pl.multiple_of(k * kstep, kstep), kstep)
        h = st[H, :, :, at].reshape(tall, kstep)
        hi = h.astype(jnp.bfloat16)
        rest = h - hi.astype(jnp.float32)
        mid = rest.astype(jnp.bfloat16)
        low = (rest - mid.astype(jnp.float32)).astype(jnp.bfloat16)
        hb[0:tall] = hi
        hb[tall : 2 * tall] = mid
        hb[2 * tall : 3 * tall] = low
        return acc + jnp.dot(hb[...], onehot[at, :], preferred_element_type=jnp.float32)

    picked = lax.fori_loop(0, cols // kstep, pick, jnp.zeros((3 * tall, n_obs), jnp.float32))
    picked = picked[0:tall] + (picked[tall : 2 * tall] + picked[2 * tall : 3 * tall])
    here = rows_of((rows, n_obs)) == obs_row
    own = jnp.zeros((PAD, n_obs), jnp.float32)
    for m in range(members):
        mine = jnp.where(here, picked[m * rows : (m + 1) * rows], 0.0)
        own = jnp.where(slot == m, jnp.sum(mine, axis=0, keepdims=True), own)
    pi[me] = own
    for peer in mates:
        tell(pi, as_sem, ar_sem, peer, me).start()
    for f in range(3):
        xb[f, me] = st[f, :, :, columns(me)]

    j = lax.shift_right_logical(rows_of((cells, np_)), int(math.log2(rows)))
    padded = j
    for k in range(1, nm):
        padded = padded + jnp.where(j >= k * members, PAD - members, 0)
    spread_rows[...] = jnp.where(lanes_of((cells, np_)) == padded, 1.0, 0.0).astype(jnp.bfloat16)

    err = flat(scale[...])
    factor = jnp.full((1, n_obs), infl[0], jnp.float32)
    known = flat(obs[...])
    weight = jnp.sqrt(factor) * err
    for peer in mates:
        tell(noise, ns_sem, nr_sem, peer, peer).wait_recv()
    aimed = known + weight * noise[...].reshape(np_, n_obs)
    for peer in mates:
        tell(pi, as_sem, ar_sem, peer, peer).wait_recv()
    predicted = pi[...].reshape(np_, n_obs)
    centre = jnp.sum(predicted, axis=0, keepdims=True) * (1.0 / total)
    inside = jnp.bitwise_and(rows_of((np_, n_obs)), PAD - 1) < members
    unit = err * norm
    spread = jnp.where(inside, (predicted - centre) / unit, 0.0)
    innovation = jnp.where(inside, (aimed - predicted) / err, 0.0)
    half = nm // 2
    core = lax.rem(me, 2)
    mine = pi[pl.ds(core * half, half)].reshape(half * PAD, n_obs)
    own_spread = jnp.where(inside[0 : half * PAD], (mine - centre) / unit, 0.0)
    zb[z] = nt(own_spread, jnp.concatenate([spread, innovation], axis=0), HIGHEST)
    others = [lax.rem(z + s, gz) for s in range(1, gz)]
    for other in others:
        share(zb, zs_sem, zr_sem, z, other, y * gz + other).start()
    for peer in mates:
        forth(V, peer, me).start()
    for peer in mates:
        forth(H, peer, me).start()
    for other in others:
        share(zb, zs_sem, zr_sem, other, other, y * gz + other).wait_recv()
    yb[y] = jnp.sum(zb[...], axis=0)
    layers = [lax.rem(y + s, gy) for s in range(1, gy)]
    for other in layers:
        share(yb, ys_sem, yr_sem, y, other, other * gz + z).start()
    for other in layers:
        share(yb, ys_sem, yr_sem, other, other, other * gz + z).wait_recv()
    sb[core] = jnp.sum(yb[...], axis=0)
    swap = pltpu.make_async_remote_copy(
        src_ref=sb.at[core], dst_ref=sb.at[core], send_sem=ss_sem, recv_sem=sr_sem,
        device_id={"mem": me + 1 - 2 * core}, device_id_type=MESH,
    )
    swap.start()
    swap.wait()

    shape = (PAD, 2 * np_)
    sub, lane = rows_of(shape), lanes_of(shape)
    blocks = [
        sb[k // half, (k % half) * PAD : (k % half + 1) * PAD]
        + jnp.where(sub + k * PAD == lane, infl[0], 0.0)
        for k in range(nm)
    ]
    for k in range(0, total, 2):
        home, r = divmod(k, members)
        p = home * PAD + r
        one, two = blocks[home][r : r + 1], blocks[home][r + 1 : r + 2]
        def lanes(x, at):
            return jnp.broadcast_to(x[:, at : at + 1], x.shape)

        a, c, d, e = lanes(one, p), lanes(one, p + 1), lanes(two, p), lanes(two, p + 1)
        scale_ = 1.0 / (a * e - c * d)
        first = (e * scale_) * one - (c * scale_) * two
        second = (a * scale_) * two - (d * scale_) * one
        new = [x - x[:, p : p + 1] * first - x[:, p + 1 : p + 2] * second for x in blocks]
        new[home] = jnp.where(sub == r, first, jnp.where(sub == r + 1, second, new[home]))
        blocks = new
    weights = jnp.concatenate([x[:, np_:] for x in blocks], axis=0)
    square = (np_, np_)
    mean = jnp.sum(weights, axis=0, keepdims=True) * (1.0 / total)
    transform = jnp.where(rows_of(square) == lanes_of(square), 1.0, 0.0) + (weights - mean) * (1.0 / norm)

    alike = jnp.bitwise_and(rows_of((cells, cells)), rows - 1) == jnp.bitwise_and(
        lanes_of((cells, cells)), rows - 1
    )

    def widen(t):
        grown = nt(spread_rows[...], t).astype(jnp.bfloat16)
        return jnp.where(alike, nt(grown, spread_rows[...]), 0.0).astype(jnp.bfloat16)

    hi = transform.astype(jnp.bfloat16)
    mix_hi = widen(hi)
    mix_lo = widen((transform - hi.astype(jnp.float32)).astype(jnp.bfloat16))

    for f in (U, H, V):
        for peer in mates:
            forth(f, peer, peer).wait_recv()
        x = xb[f].reshape(cells, width)
        x_hi = x.astype(jnp.bfloat16)
        x_lo = (x - x_hi.astype(jnp.float32)).astype(jnp.bfloat16)
        mixed = jnp.dot(mix_hi, x_hi, preferred_element_type=jnp.float32) + (
            jnp.dot(mix_hi, x_lo, preferred_element_type=jnp.float32)
            + jnp.dot(mix_lo, x_hi, preferred_element_type=jnp.float32)
        )
        mb[f] = mixed.reshape(nm, members, rows, width)
        if f == V:
            for peer in mates:
                back(H, peer, me).wait_send()
        for peer in mates:
            back(f, peer, me).start()
        out[:, f, :, columns(me)] = mb[f, me]

    for peer in mates:
        back(H, peer, peer).wait_recv()

    @pl.loop(0, members)
    def _(m):
        edges(3, m, out[m, H])

    for peer in mates:
        back(U, peer, peer).wait_recv()

    @pl.loop(0, members)
    def _(m):
        out[m, U] = out[m, U] - 0.25 * east(out[m, H])

    @pl.loop(0, members)
    def _(m):
        arrive(3, m)
        dv[m] = 0.25 * north(out[m, H], hr[3, 0, m], hr[3, 1, m])

    def finish(src):
        at = columns(src)
        f = turn(width)
        for m in range(members):
            v = out[m, V, :, at]
            u = out[m, U, :, at] + f * v
            out[m, U, :, at] = u
            out[m, V, :, at] = v - dv[m, :, at] - f * u

    finish(me)

    @pl.loop(1, nm)
    def _(s):
        peer = lax.rem(me + s, nm)
        back(V, peer, peer).wait_recv()
        finish(peer)

    @pl.loop(0, members)
    def _(m):
        for t in range(4):

            @pl.when(b > 0)
            def _():
                halo(t, 0, m).wait_send()

            @pl.when(b < nb - 1)
            def _():
                halo(t, 1, m).wait_send()

    for peer in mates:
        tell(noise, ns_sem, nr_sem, peer, me).wait_send()
        tell(pi, as_sem, ar_sem, peer, me).wait_send()
    for other in others:
        share(zb, zs_sem, zr_sem, z, other, y * gz + other).wait_send()
    for other in layers:
        share(yb, ys_sem, yr_sem, y, other, other * gz + z).wait_send()
    for peer in mates:
        for f in range(3):
            forth(f, peer, me).wait_send()
        back(U, peer, me).wait_send()
        back(V, peer, me).wait_send()


def body(ens, depth, pos, obs, scale, pert, infl):
    nm, nb = lax.axis_size("mem"), lax.axis_size("band")
    gz = 8 if nb >= 16 else 2
    gy = nb // gz
    members, fields, rows, cols = ens.shape
    n_obs = pos.size
    np_ = nm * PAD
    cells = nm * members * rows
    f32, bf16 = jnp.float32, jnp.bfloat16
    dma = pltpu.SemaphoreType.DMA
    vmem = pl.BlockSpec(memory_space=pltpu.VMEM)
    return pl.pallas_call(
        functools.partial(kernel, nm, nb, gz),
        out_shape=jax.ShapeDtypeStruct(ens.shape, f32),
        in_specs=[pl.BlockSpec(memory_space=pltpu.HBM)] * 6 + [pl.BlockSpec(memory_space=pltpu.SMEM)],
        out_specs=vmem,
        scratch_shapes=[
            pltpu.VMEM(depth.shape, f32),
            pltpu.VMEM(pos.shape, jnp.int32),
            pltpu.VMEM(obs.shape, f32),
            pltpu.VMEM(scale.shape, f32),
            pltpu.VMEM(pert.shape, f32),
            pltpu.VMEM((fields, members, rows, cols), f32),
            pltpu.VMEM((members, rows, cols), f32),
            pltpu.VMEM((4, 2, members, 1, cols), f32),
            pltpu.VMEM((4, 2, members, 1, cols), f32),
            pltpu.VMEM((cols, n_obs), bf16),
            pltpu.VMEM((3 * members * rows, cols // 2), bf16),
            pltpu.VMEM((nm, PAD, n_obs), f32),
            pltpu.VMEM((nm, PAD, n_obs), f32),
            pltpu.VMEM((gz, np_ // 2, 2 * np_), f32),
            pltpu.VMEM((gy, np_ // 2, 2 * np_), f32),
            pltpu.VMEM((2, np_ // 2, 2 * np_), f32),
            pltpu.VMEM((fields, nm, members, rows, cols // nm), f32),
            pltpu.VMEM((fields, nm, members, rows, cols // nm), f32),
            pltpu.VMEM((cells, np_), bf16),
            dma((fields,)),
            dma((5,)),
            dma((4, 2, members)),
            dma((4, 2, members)),
            dma((nm,)),
            dma((nm,)),
            dma((nm,)),
            dma((nm,)),
            dma((gz,)),
            dma((gz,)),
            dma((gy,)),
            dma((gy,)),
            dma,
            dma,
            dma((fields, nm)),
            dma((fields, nm)),
            dma((fields, nm)),
            dma((fields, nm)),
        ],
        compiler_params=pltpu.CompilerParams(
            collective_id=0, has_side_effects=True, vmem_limit_bytes=48 * 1024 * 1024
        ),
        name="smoother",
    )(*[pltpu.with_memory_space_constraint(x, pltpu.HBM) for x in (ens, depth, pos, obs, scale, pert)], infl)


def solution(mesh):
    in_specs = (
        P("mem", None, "band", None),
        P("band", None),
        P("band", None),
        P("band", None),
        P("band", None),
        P("mem", "band", None),
        P(),
    )
    out_specs = P("mem", None, "band", None)
    return jax.shard_map(body, mesh=mesh, in_specs=in_specs, out_specs=out_specs, check_vma=False)
```

```python
import functools
import math

import jax
import jax.numpy as jnp
from jax import lax
from jax.experimental import pallas as pl
from jax.experimental.pallas import tpu as pltpu
from jax.sharding import PartitionSpec as P

MESH = pl.DeviceIdType.MESH
HIGHEST = lax.Precision.HIGHEST

coriolis_base = 0.15
coriolis_slope = 0.3
PAD = 8


def rows_of(shape):
    return lax.broadcasted_iota(jnp.int32, shape, 0)


def lanes_of(shape):
    return lax.broadcasted_iota(jnp.int32, shape, 1)


def east(q):
    n = q.shape[1]
    return pltpu.roll(q, n - 1, 1) - pltpu.roll(q, 1, 1)


def north(q, above, below):
    n = q.shape[0]
    row = rows_of(q.shape)
    after = jnp.where(row == n - 1, below, pltpu.roll(q, n - 1, 0))
    before = jnp.where(row == 0, above, pltpu.roll(q, 1, 0))
    return after - before


def nt(a, b, precision=None):
    return lax.dot_general(
        a, b, (((1,), (1,)), ((), ())), precision=precision, preferred_element_type=jnp.float32
    )


def kernel(
    nm, nb, gz,
    ens, depth_in, pos_in, obs_in, scale_in, pert_in, infl,
    out,
    depth, pos, obs, scale, pert,
    st, dv, hs, hr, onehot, hb, noise, pi, zb, yb, sb, xb, mb, spread_rows,
    load_sem, small_sem, hs_sem, hr_sem, ns_sem, nr_sem, as_sem, ar_sem, zs_sem, zr_sem, ys_sem, yr_sem,
    ss_sem, sr_sem, fs_sem, fr_sem, bs_sem, br_sem,
):
    _, members, rows, cols = st.shape
    n_obs = onehot.shape[1]
    width = cols // nm
    np_ = nm * PAD
    total = nm * members
    cells = total * rows
    gy = nb // gz
    norm = math.sqrt(total - 1)
    H, U, V = 0, 1, 2
    me, b = lax.axis_index("mem"), lax.axis_index("band")
    z, y = lax.rem(b, gz), lax.div(b, gz)
    mates = [lax.rem(me + s, nm) for s in range(1, nm)]

    small = [
        pltpu.make_async_copy(source, target, small_sem.at[k])
        for k, (source, target) in enumerate(
            [(depth_in, depth), (pos_in, pos), (obs_in, obs), (scale_in, scale), (pert_in, pert)]
        )
    ]
    load = [pltpu.make_async_copy(ens.at[:, f], st.at[f], load_sem.at[f]) for f in range(3)]
    small[0].start()
    load[V].start()
    small[4].start()
    load[U].start()
    load[H].start()
    for copy in small[1:4]:
        copy.start()

    barrier = pltpu.get_barrier_semaphore()

    def greet(where):
        pl.semaphore_signal(barrier, 1, device_id=where, device_id_type=MESH)

    for peer in mates:
        greet({"mem": peer})
    for s in range(1, gz):
        greet({"band": y * gz + lax.rem(z + s, gz)})
    for s in range(1, gy):
        greet({"band": lax.rem(y + s, gy) * gz + z})
    far_above = jnp.logical_and(z == 0, y > 0)
    far_below = jnp.logical_and(z == gz - 1, y < gy - 1)

    @pl.when(far_above)
    def _():
        greet({"band": b - 1})

    @pl.when(far_below)
    def _():
        greet({"band": b + 1})

    @pl.when(b == 0)
    def _():
        hr[:, 0] = jnp.zeros_like(hr[:, 0])

    @pl.when(b == nb - 1)
    def _():
        hr[:, 1] = jnp.zeros_like(hr[:, 1])

    def turn(lanes):
        row = (rows_of((rows, lanes)) + b * rows).astype(jnp.float32)
        return coriolis_base + coriolis_slope * (row + 0.5) / (nb * rows)

    def halo(t, side, m):
        return pltpu.make_async_remote_copy(
            src_ref=hs.at[t, side, m],
            dst_ref=hr.at[t, 1 - side, m],
            send_sem=hs_sem.at[t, side, m],
            recv_sem=hr_sem.at[t, 1 - side, m],
            device_id={"band": jnp.where(b > 0, b - 1, 0) if side == 0 else jnp.where(b < nb - 1, b + 1, b)},
            device_id_type=MESH,
        )

    def edges(t, m, q):
        hs[t, 0, m] = q[0:1]
        hs[t, 1, m] = q[rows - 1 : rows]

        @pl.when(b > 0)
        def _():
            halo(t, 0, m).start()

        @pl.when(b < nb - 1)
        def _():
            halo(t, 1, m).start()

    def arrive(t, m):
        @pl.when(b > 0)
        def _():
            halo(t, 1, m).wait_recv()

        @pl.when(b < nb - 1)
        def _():
            halo(t, 0, m).wait_recv()

    def tell(buf, send, recv, peer, src):
        return pltpu.make_async_remote_copy(
            src_ref=buf.at[src], dst_ref=buf.at[src], send_sem=send.at[peer],
            recv_sem=recv.at[src], device_id={"mem": peer}, device_id_type=MESH,
        )

    def share(buf, send, recv, slot, other, peer):
        return pltpu.make_async_remote_copy(
            src_ref=buf.at[slot], dst_ref=buf.at[slot], send_sem=send.at[other],
            recv_sem=recv.at[slot], device_id={"band": peer}, device_id_type=MESH,
        )

    def columns(peer):
        return pl.ds(pl.multiple_of(peer * width, width), width)

    def forth(f, peer, src):
        return pltpu.make_async_remote_copy(
            src_ref=st.at[f, :, :, columns(peer)], dst_ref=xb.at[f, src], send_sem=fs_sem.at[f, peer],
            recv_sem=fr_sem.at[f, src], device_id={"mem": peer}, device_id_type=MESH,
        )

    def forth_one(f, m, peer):
        return pltpu.make_async_remote_copy(
            src_ref=st.at[f, m, :, columns(peer)], dst_ref=xb.at[f, me, m], send_sem=fs_sem.at[f, peer],
            recv_sem=fr_sem.at[f, me], device_id={"mem": peer}, device_id_type=MESH,
        )

    def back(f, peer, src):
        return pltpu.make_async_remote_copy(
            src_ref=mb.at[f, peer], dst_ref=out.at[:, f, :, columns(src)], send_sem=bs_sem.at[f, peer],
            recv_sem=br_sem.at[f, src], device_id={"mem": peer}, device_id_type=MESH,
        )

    pl.semaphore_wait(
        barrier,
        nm - 1 + gz - 1 + gy - 1 + jnp.where(far_above, 1, 0) + jnp.where(far_below, 1, 0),
    )

    small[0].wait()
    load[V].wait()

    @pl.loop(0, members)
    def _(m):
        flux = depth[...] * st[V, m]
        dv[m] = flux
        edges(0, m, flux)

    def flat(x):
        return jnp.concatenate([x[q : q + 1, :] for q in range(x.shape[0])], axis=1)

    small[4].wait()
    slot = rows_of((PAD, n_obs))
    own_noise = jnp.zeros((PAD, n_obs), jnp.float32)
    for m in range(members):
        own_noise = jnp.where(slot == m, flat(pert[m]), own_noise)
    noise[me] = own_noise
    for peer in mates:
        tell(noise, ns_sem, nr_sem, peer, me).start()

    load[U].wait()
    load[H].wait()

    @pl.loop(0, members)
    def _(m):
        st[H, m] = st[H, m] - 0.25 * east(depth[...] * st[U, m])

    @pl.loop(0, members)
    def _(m):
        arrive(0, m)
        h = st[H, m] - 0.25 * north(dv[m], hr[0, 0, m], hr[0, 1, m])
        st[H, m] = h
        edges(1, m, h)
        st[U, m] = st[U, m] - 0.25 * east(h) + turn(cols) * st[V, m]
        for peer in mates:
            forth_one(U, m, peer).start()

    for copy in small[1:4]:
        copy.wait()

    local = flat(pos[...]) - b * (rows * cols)
    obs_row = lax.shift_right_logical(local, int(math.log2(cols)))
    obs_col = jnp.bitwise_and(local, cols - 1)
    step = 256

    @pl.loop(0, cols // step)
    def _(k):
        col = rows_of((step, n_obs)) + k * step
        onehot[pl.ds(pl.multiple_of(k * step, step), step), :] = jnp.where(
            col == obs_col, 1.0, 0.0
        ).astype(jnp.bfloat16)

    @pl.loop(0, members)
    def _(m):
        arrive(1, m)
        v = st[V, m] - 0.25 * north(st[H, m], hr[1, 0, m], hr[1, 1, m]) - turn(cols) * st[U, m]
        st[V, m] = v
        flux = depth[...] * v
        dv[m] = flux
        edges(2, m, flux)

    @pl.loop(0, members)
    def _(m):
        h = st[H, m] - 0.25 * east(depth[...] * st[U, m])
        arrive(2, m)
        st[H, m] = h - 0.25 * north(dv[m], hr[2, 0, m], hr[2, 1, m])

    tall = members * rows
    kstep = cols

    def pick(k, acc):
        at = pl.ds(pl.multiple_of(k * kstep, kstep), kstep)
        h = st[H, :, :, at].reshape(tall, kstep)
        hi = h.astype(jnp.bfloat16)
        rest = h - hi.astype(jnp.float32)
        mid = rest.astype(jnp.bfloat16)
        low = (rest - mid.astype(jnp.float32)).astype(jnp.bfloat16)
        hb[0:tall] = hi
        hb[tall : 2 * tall] = mid
        hb[2 * tall : 3 * tall] = low
        return acc + jnp.dot(hb[...], onehot[at, :], preferred_element_type=jnp.float32)

    picked = lax.fori_loop(0, cols // kstep, pick, jnp.zeros((3 * tall, n_obs), jnp.float32))
    picked = picked[0:tall] + (picked[tall : 2 * tall] + picked[2 * tall : 3 * tall])
    here = rows_of((rows, n_obs)) == obs_row
    own = jnp.zeros((PAD, n_obs), jnp.float32)
    for m in range(members):
        mine = jnp.where(here, picked[m * rows : (m + 1) * rows], 0.0)
        own = jnp.where(slot == m, jnp.sum(mine, axis=0, keepdims=True), own)
    pi[me] = own
    for peer in mates:
        tell(pi, as_sem, ar_sem, peer, me).start()
    for f in range(3):
        xb[f, me] = st[f, :, :, columns(me)]

    j = lax.shift_right_logical(rows_of((cells, np_)), int(math.log2(rows)))
    padded = j
    for k in range(1, nm):
        padded = padded + jnp.where(j >= k * members, PAD - members, 0)
    spread_rows[...] = jnp.where(lanes_of((cells, np_)) == padded, 1.0, 0.0).astype(jnp.bfloat16)

    err = flat(scale[...])
    factor = jnp.full((1, n_obs), infl[0], jnp.float32)
    known = flat(obs[...])
    weight = jnp.sqrt(factor) * err
    for peer in mates:
        tell(noise, ns_sem, nr_sem, peer, peer).wait_recv()
    aimed = known + weight * noise[...].reshape(np_, n_obs)
    for peer in mates:
        tell(pi, as_sem, ar_sem, peer, peer).wait_recv()
    predicted = pi[...].reshape(np_, n_obs)
    centre = jnp.sum(predicted, axis=0, keepdims=True) * (1.0 / total)
    inside = jnp.bitwise_and(rows_of((np_, n_obs)), PAD - 1) < members
    unit = err * norm
    spread = jnp.where(inside, (predicted - centre) / unit, 0.0)
    innovation = jnp.where(inside, (aimed - predicted) / err, 0.0)
    half = nm // 2
    core = lax.rem(me, 2)
    mine = pi[pl.ds(core * half, half)].reshape(half * PAD, n_obs)
    own_spread = jnp.where(inside[0 : half * PAD], (mine - centre) / unit, 0.0)
    zb[z] = nt(own_spread, jnp.concatenate([spread, innovation], axis=0), HIGHEST)
    others = [lax.rem(z + s, gz) for s in range(1, gz)]
    for other in others:
        share(zb, zs_sem, zr_sem, z, other, y * gz + other).start()
    for peer in mates:
        forth(V, peer, me).start()
    for peer in mates:
        forth(H, peer, me).start()
    for other in others:
        share(zb, zs_sem, zr_sem, other, other, y * gz + other).wait_recv()
    yb[y] = jnp.sum(zb[...], axis=0)
    layers = [lax.rem(y + s, gy) for s in range(1, gy)]
    for other in layers:
        share(yb, ys_sem, yr_sem, y, other, other * gz + z).start()
    for other in layers:
        share(yb, ys_sem, yr_sem, other, other, other * gz + z).wait_recv()
    sb[core] = jnp.sum(yb[...], axis=0)
    swap = pltpu.make_async_remote_copy(
        src_ref=sb.at[core], dst_ref=sb.at[core], send_sem=ss_sem, recv_sem=sr_sem,
        device_id={"mem": me + 1 - 2 * core}, device_id_type=MESH,
    )
    swap.start()
    swap.wait()

    shape = (PAD, 2 * np_)
    sub, lane = rows_of(shape), lanes_of(shape)
    blocks = [
        sb[k // half, (k % half) * PAD : (k % half + 1) * PAD]
        + jnp.where(sub + k * PAD == lane, infl[0], 0.0)
        for k in range(nm)
    ]
    for k in range(0, total, 2):
        home, r = divmod(k, members)
        p = home * PAD + r
        one, two = blocks[home][r : r + 1], blocks[home][r + 1 : r + 2]
        def lanes(x, at):
            return jnp.broadcast_to(x[:, at : at + 1], x.shape)

        a, c, d, e = lanes(one, p), lanes(one, p + 1), lanes(two, p), lanes(two, p + 1)
        scale_ = 1.0 / (a * e - c * d)
        first = (e * scale_) * one - (c * scale_) * two
        second = (a * scale_) * two - (d * scale_) * one
        new = [x - x[:, p : p + 1] * first - x[:, p + 1 : p + 2] * second for x in blocks]
        new[home] = jnp.where(sub == r, first, jnp.where(sub == r + 1, second, new[home]))
        blocks = new
    weights = jnp.concatenate([x[:, np_:] for x in blocks], axis=0)
    square = (np_, np_)
    mean = jnp.sum(weights, axis=0, keepdims=True) * (1.0 / total)
    transform = jnp.where(rows_of(square) == lanes_of(square), 1.0, 0.0) + (weights - mean) * (1.0 / norm)

    alike = jnp.bitwise_and(rows_of((cells, cells)), rows - 1) == jnp.bitwise_and(
        lanes_of((cells, cells)), rows - 1
    )

    def widen(t):
        grown = nt(spread_rows[...], t).astype(jnp.bfloat16)
        return jnp.where(alike, nt(grown, spread_rows[...]), 0.0).astype(jnp.bfloat16)

    hi = transform.astype(jnp.bfloat16)
    mix_hi = widen(hi)
    mix_lo = widen((transform - hi.astype(jnp.float32)).astype(jnp.bfloat16))

    for f in (U, H, V):
        for peer in mates:
            forth(f, peer, peer).wait_recv()
        x = xb[f].reshape(cells, width)
        x_hi = x.astype(jnp.bfloat16)
        x_lo = (x - x_hi.astype(jnp.float32)).astype(jnp.bfloat16)
        mixed = jnp.dot(mix_hi, x_hi, preferred_element_type=jnp.float32) + (
            jnp.dot(mix_hi, x_lo, preferred_element_type=jnp.float32)
            + jnp.dot(mix_lo, x_hi, preferred_element_type=jnp.float32)
        )
        mb[f] = mixed.reshape(nm, members, rows, width)
        if f == V:
            for peer in mates:
                back(H, peer, me).wait_send()
        for peer in mates:
            back(f, peer, me).start()
        out[:, f, :, columns(me)] = mb[f, me]

    for peer in mates:
        back(H, peer, peer).wait_recv()

    @pl.loop(0, members)
    def _(m):
        edges(3, m, out[m, H])

    for peer in mates:
        back(U, peer, peer).wait_recv()

    @pl.loop(0, members)
    def _(m):
        out[m, U] = out[m, U] - 0.25 * east(out[m, H])

    @pl.loop(0, members)
    def _(m):
        arrive(3, m)
        dv[m] = 0.25 * north(out[m, H], hr[3, 0, m], hr[3, 1, m])

    def finish(src):
        at = columns(src)
        f = turn(width)
        for m in range(members):
            v = out[m, V, :, at]
            u = out[m, U, :, at] + f * v
            out[m, U, :, at] = u
            out[m, V, :, at] = v - dv[m, :, at] - f * u

    finish(me)

    @pl.loop(1, nm)
    def _(s):
        peer = lax.rem(me + s, nm)
        back(V, peer, peer).wait_recv()
        finish(peer)

    @pl.loop(0, members)
    def _(m):
        for t in range(4):

            @pl.when(b > 0)
            def _():
                halo(t, 0, m).wait_send()

            @pl.when(b < nb - 1)
            def _():
                halo(t, 1, m).wait_send()

    for peer in mates:
        tell(noise, ns_sem, nr_sem, peer, me).wait_send()
        tell(pi, as_sem, ar_sem, peer, me).wait_send()
    for other in others:
        share(zb, zs_sem, zr_sem, z, other, y * gz + other).wait_send()
    for other in layers:
        share(yb, ys_sem, yr_sem, y, other, other * gz + z).wait_send()
    for peer in mates:
        for f in range(3):
            forth(f, peer, me).wait_send()
        back(U, peer, me).wait_send()
        back(V, peer, me).wait_send()


def body(ens, depth, pos, obs, scale, pert, infl):
    nm, nb = lax.axis_size("mem"), lax.axis_size("band")
    gz = 8 if nb >= 16 else 2
    gy = nb // gz
    members, fields, rows, cols = ens.shape
    n_obs = pos.size
    np_ = nm * PAD
    cells = nm * members * rows
    f32, bf16 = jnp.float32, jnp.bfloat16
    dma = pltpu.SemaphoreType.DMA
    vmem = pl.BlockSpec(memory_space=pltpu.VMEM)
    return pl.pallas_call(
        functools.partial(kernel, nm, nb, gz),
        out_shape=jax.ShapeDtypeStruct(ens.shape, f32),
        in_specs=[pl.BlockSpec(memory_space=pltpu.HBM)] * 6 + [pl.BlockSpec(memory_space=pltpu.SMEM)],
        out_specs=vmem,
        scratch_shapes=[
            pltpu.VMEM(depth.shape, f32),
            pltpu.VMEM(pos.shape, jnp.int32),
            pltpu.VMEM(obs.shape, f32),
            pltpu.VMEM(scale.shape, f32),
            pltpu.VMEM(pert.shape, f32),
            pltpu.VMEM((fields, members, rows, cols), f32),
            pltpu.VMEM((members, rows, cols), f32),
            pltpu.VMEM((4, 2, members, 1, cols), f32),
            pltpu.VMEM((4, 2, members, 1, cols), f32),
            pltpu.VMEM((cols, n_obs), bf16),
            pltpu.VMEM((3 * members * rows, cols), bf16),
            pltpu.VMEM((nm, PAD, n_obs), f32),
            pltpu.VMEM((nm, PAD, n_obs), f32),
            pltpu.VMEM((gz, np_ // 2, 2 * np_), f32),
            pltpu.VMEM((gy, np_ // 2, 2 * np_), f32),
            pltpu.VMEM((2, np_ // 2, 2 * np_), f32),
            pltpu.VMEM((fields, nm, members, rows, cols // nm), f32),
            pltpu.VMEM((fields, nm, members, rows, cols // nm), f32),
            pltpu.VMEM((cells, np_), bf16),
            dma((fields,)),
            dma((5,)),
            dma((4, 2, members)),
            dma((4, 2, members)),
            dma((nm,)),
            dma((nm,)),
            dma((nm,)),
            dma((nm,)),
            dma((gz,)),
            dma((gz,)),
            dma((gy,)),
            dma((gy,)),
            dma,
            dma,
            dma((fields, nm)),
            dma((fields, nm)),
            dma((fields, nm)),
            dma((fields, nm)),
        ],
        compiler_params=pltpu.CompilerParams(
            collective_id=0, has_side_effects=True, vmem_limit_bytes=48 * 1024 * 1024
        ),
        name="smoother",
    )(*[pltpu.with_memory_space_constraint(x, pltpu.HBM) for x in (ens, depth, pos, obs, scale, pert)], infl)


def solution(mesh):
    in_specs = (
        P("mem", None, "band", None),
        P("band", None),
        P("band", None),
        P("band", None),
        P("band", None),
        P("mem", "band", None),
        P(),
    )
    out_specs = P("mem", None, "band", None)
    return jax.shard_map(body, mesh=mesh, in_specs=in_specs, out_specs=out_specs, check_vma=False)
```
